768 devices in a mesh: along: 96 (over x, z, core), across: 8 (over y).
Axes of the slice: x: 4, y: 8, z: 12, core: 2. Of those that a mesh axis runs over, the one named last changes fastest.
Arguments:
- field_now: float32 [3072, 256, 128], P('along', 'across'), may hold values from -6 to 6
- field_before: float32 [3072, 256, 128], P('along', 'across'), may hold values from -6 to 6
- layer: int32 [3072, 256, 128], P('along', 'across'), may hold values from 0 to 7
- modulus_table: float32 [8], replicated, may hold values from 0.4 to 2
- fk_panel: bfloat16 [2, 192, 8, 12288], P(None, 'along', 'across'), may hold values from -6 to 6
- owner: int32 [8, 12288, 1], P('across', 'along'), may hold values from 0 to 7; in each aligned block of 128 rows (0 to 127, 128 to 255, ..., all dimensions but the last counted through in order) at most 64 rows name the same one
- local_cell: int32 [8, 12288], P('across', 'along'), may hold values from 0 to 131071
Outputs:
- field_next: float32 [3072, 256, 128], P('along', 'across')
- field_prior: float32 [3072, 256, 128], P('along', 'across')
The draws below stay inside these ranges and needn't reach their ends.
Inputs may be any that keep to these rules, and one draw needn't show every extreme that they name: Among the 128 points of one tile (one row of owner and column block of 128), at most 64 have the same owner, and this many is reached.
All inputs are finite; a program needn't handle non-finite values.
Results may differ from the reference program's by a relative error of at most 0.0003.
Values may be sent and summed in bfloat16 or wider, within the bound.
No kernel may reach another device: no remote copies, remote signals or barrier semaphores. Data moves between devices by JAX's collectives and lax.ppermute only.
A program may use at most 192 MiB of HBM per device.

```python
import math
import jax
import jax.numpy as jnp
import numpy as np
from jax import lax

CX = 32
CY = 32
CZ = 128
P_DEV = 128
STEPS = 8
LAYERS = 8
TILES_Y = 8
FREQS = 192
PTS_ROW = 12288
CAP = 64
CELLS = 131072
NX = 3072
NY = 256


def set_ends(entries, own_key, least, largest):
    longest = entries.shape.index(max(entries.shape))
    spots = []
    for shift in (0, 1):
        where = [jax.random.randint(jax.random.fold_in(own_key, axis), (), 0, length) for axis, length in enumerate(entries.shape)]
        where[longest] = (where[longest] + shift) % entries.shape[longest]
        spots.append(tuple(where))
    return entries.at[spots[0]].set(least).at[spots[1]].set(largest)


def block_levels(key, extent, pieces, least, top_value):
    def one(position, shards_of):
        steps = jax.random.uniform(jax.random.fold_in(jax.random.fold_in(key, 6), position), (shards_of,), jnp.float32, least / len(pieces), top_value / len(pieces))
        return jnp.repeat(jnp.exp(steps), extent[position] // shards_of).reshape((-1,) + (1,) * (len(extent) - position - 1))

    gain = one(*pieces[0])
    for cut in pieces[1:]:
        gain = gain * one(*cut)
    return gain


def deal_out(own_key, own, number, rows, number_of, top, bound, lean):
    order = jax.random.permutation(own_key, number_of)
    crowded, common = load_shares(number_of, rows * top, bound, lean, True), load_shares(number_of, rows * top, bound, lean, False)
    places = jnp.arange(number_of)

    def named(tallies, offset_by):
        used = int((tallies > 0).sum())
        fixed = max(1, used // 4)
        moved = fixed + (places - fixed + offset_by * (used - fixed)) % max(1, number_of - fixed)
        return jnp.zeros((number_of,), jnp.int32).at[order[jnp.where(places < fixed, places, moved)]].set(jnp.asarray(tallies, jnp.int32))

    tallies = jnp.where(number % 4 == 0, named(crowded, number // 4), named(common, number - number // 4 - 1))
    mixed = jax.random.permutation(jax.random.fold_in(own, 3), number_of)
    source_of, taker = mixed[0:number_of // 2 * 2:2], mixed[1:number_of // 2 * 2:2]
    slack = jnp.minimum(tallies[source_of] - 1, bound - tallies[taker]) // 2
    slack = jnp.where((source_of == order[0]) | (taker == order[0]) | (tallies[taker] == 0), 0, jnp.maximum(slack, 0))
    moved = jax.random.randint(jax.random.fold_in(own, 4), (number_of // 2,), 0, 1 << 20) % (slack + 1)
    tallies = tallies.at[source_of].add(-moved).at[taker].add(moved)
    members = jnp.searchsorted(jnp.cumsum(tallies), jnp.arange(rows * top), side="right").astype(jnp.int32)
    table = members.reshape(top, rows).T
    table = table[jax.random.permutation(jax.random.fold_in(own, 1), rows)]
    offset_by = jax.random.randint(jax.random.fold_in(own, 2), (rows, 1), 0, top)
    return jnp.take_along_axis(table, (jnp.arange(top)[None, :] + offset_by) % top, axis=1)


def load_shares(number_of, total, reach, lean, full):
    portions = [(1 << 20) // math.isqrt(grade ** lean) + 1 for grade in range(1, number_of + 1)]
    largest = reach if full else min(reach, max(-(-total // number_of), total * portions[0] // sum(portions)))
    least = 1 if total - largest >= number_of - 1 else 0
    counts, spare = [largest] + [least] * (number_of - 1), total - largest - least * (number_of - 1)
    while spare > 0:
        free = [i for i in range(1, number_of) if counts[i] < largest] or [i for i in range(1, number_of) if counts[i] < reach]
        pool, budget = sum([portions[i] for i in free]), spare
        for i in free:
            addition = min(reach - counts[i], max(1, budget * portions[i] // pool), spare)
            counts[i] = counts[i] + addition
            spare = spare - addition
    return np.array(counts)


def noise(own_key, shape, spread, limit, cuts=(), kind=jnp.bfloat16):
    factor_of = block_levels(own_key, shape, cuts, -0.22, 0.18) if cuts else 1.0
    drawn = jax.random.normal(own_key, shape, jnp.float32) * spread * factor_of
    return jnp.minimum(jnp.maximum(drawn, -limit), limit).astype(kind)


def setup_inputs(seed: int = 0) -> dict:
    key_of = jax.random.split(jax.random.key(seed), 8)
    field_now = noise(key_of[0], (NX, NY, CZ), 1.0, 6.0, ((0, 96), (1, 8)), jnp.float32)
    field_before = noise(key_of[1], (NX, NY, CZ), 1.0, 6.0, ((0, 96), (1, 8)), jnp.float32)
    layer = set_ends(jax.random.randint(key_of[2], (NX, NY, CZ), 0, LAYERS), jax.random.fold_in(key_of[2], 1), 0, LAYERS - 1).astype(jnp.int32)
    modulus_table = jnp.clip(jnp.exp(jax.random.uniform(key_of[3], (LAYERS,), jnp.float32, math.log(0.4), math.log(2.0))), 0.4, 2.0)
    fk_panel = noise(key_of[4], (2, FREQS, TILES_Y, PTS_ROW), 1.0, 6.0, ((1, 96), (2, 8)))
    owner_keys = jax.random.split(jax.random.fold_in(key_of[5], 1), TILES_Y * PTS_ROW // P_DEV)
    owner_turns = jax.random.permutation(jax.random.fold_in(key_of[5], 3), TILES_Y * PTS_ROW // P_DEV)
    owner = jax.vmap(lambda own, number: deal_out(jax.random.fold_in(key_of[5], 2), own, number, P_DEV, TILES_Y, 1, CAP, 2))(owner_keys, owner_turns).reshape((TILES_Y, PTS_ROW, 1))
    local_cell = set_ends(jax.random.randint(key_of[6], (TILES_Y, PTS_ROW), 0, CELLS), jax.random.fold_in(key_of[6], 1), 0, CELLS - 1).astype(jnp.int32)
    return {"field_now": field_now, "field_before": field_before, "layer": layer, "modulus_table": modulus_table, "fk_panel": fk_panel, "owner": owner, "local_cell": local_cell}


def stiffness(u_pad, mu_pad):
    uc = u_pad[1:-1, 1:-1, 1:-1]
    mc = mu_pad[1:-1, 1:-1, 1:-1]
    total = jnp.zeros_like(uc)
    for sx, sy, sz in ((2, 1, 1), (0, 1, 1), (1, 2, 1), (1, 0, 1), (1, 1, 2), (1, 1, 0)):
        ex = u_pad.shape[0] - 2 + sx
        ey = u_pad.shape[1] - 2 + sy
        ez = u_pad.shape[2] - 2 + sz
        un = u_pad[sx:ex, sy:ey, sz:ez]
        mn = mu_pad[sx:ex, sy:ey, sz:ez]
        total = total + 0.5 * (mc + mn) * (un - uc)
    return total

def reference(field_now, field_before, layer, modulus_table, fk_panel, owner, local_cell):
    modulus = modulus_table[layer].astype(jnp.float32)
    mu_pad = jnp.pad(modulus, 1)
    freq = jnp.arange(FREQS).astype(jnp.float32)
    times = jnp.arange(STEPS).astype(jnp.float32)
    phase = math.pi * times[:, None] * freq[None, :] / FREQS
    table = jnp.concatenate([jnp.cos(phase), -jnp.sin(phase)], axis=1) / math.sqrt(FREQS)
    points = TILES_Y * PTS_ROW
    panel = fk_panel.astype(jnp.float32).reshape(2 * FREQS, points)
    forcing = jnp.dot(table, panel, precision=lax.Precision.HIGHEST)
    owner_flat = owner.reshape(points).astype(jnp.int32)
    cell_flat = local_cell.reshape(points).astype(jnp.int32)
    column = jnp.arange(points, dtype=jnp.int32) % PTS_ROW
    grid_x = column // P_DEV * CX + cell_flat // (CY * CZ)
    grid_y = owner_flat * CY + cell_flat // CZ % CY
    grid_z = cell_flat % CZ
    now, before = (field_now, field_before)
    for step in range(STEPS):
        drive = jnp.zeros(now.shape, jnp.float32).at[grid_x, grid_y, grid_z].add(forcing[step])
        new = 2.0 * now - before + 0.15 * stiffness(jnp.pad(now, 1), mu_pad) + drive
        before = now
        now = new
    return (now, before)
```

```python
import math

import jax
import jax.numpy as jnp
import ml_dtypes
import numpy as np
from jax import lax
from jax.experimental import pallas as pl
from jax.experimental.pallas import tpu as pltpu
from jax.sharding import PartitionSpec as P

STEPS = 8
H = 8
CX, CY, CZ = 32, 32, 128
EX, EY = CX + 2 * H, CY + 2 * H
PY = EY + 2 * H
ROWS = EX * EY
CELLS = CX * CY * CZ
NPT = 128
ROW_BITS, Z_BITS, P_BITS = 12, 7, 12
LIMIT = 56 * 1024 * 1024


def vmem_spec():
    return pl.BlockSpec(memory_space=pltpu.VMEM)


def any_spec():
    return pl.BlockSpec(memory_space=pl.ANY)


def split_table(sources, local_freqs):
    total = sources * local_freqs
    freq = np.arange(total, dtype=np.float64).reshape(sources, 1, local_freqs)
    times = np.arange(STEPS, dtype=np.float64).reshape(STEPS, 1, 1, 1)
    phase = math.pi * times * freq[None] / total
    table = np.concatenate([np.cos(phase), -np.sin(phase)], axis=2) / math.sqrt(total)
    rest = table.reshape(STEPS, 2 * total).astype(np.float32)
    parts = []
    for _ in range(3):
        part = rest.astype(ml_dtypes.bfloat16)
        parts.append(part)
        rest = rest - part.astype(np.float32)
    return np.concatenate(parts, axis=0)


def deal_kernel(fk_ref, out_ref):
    for i in range(out_ref.shape[0]):
        for c in range(2):
            out_ref[i, pl.ds(2 * c, 2), :] = fk_ref[c, :, pl.ds(i * NPT, NPT)]


def transform_kernel(moved_ref, table_ref, owner_ref, cell_ref, out_ref, wide_ref):
    for i in range(moved_ref.shape[0]):
        wide_ref[pl.ds(4 * i, 4), :] = moved_ref[i].astype(jnp.float32)
    panel = wide_ref[...].astype(jnp.bfloat16)
    parts = jnp.dot(table_ref[...], panel, preferred_element_type=jnp.float32)
    force = parts[0:8] + parts[8:16] + parts[16:24]
    key = (owner_ref[...] * CELLS + cell_ref[...] + 1).astype(jnp.float32)
    keys = jnp.broadcast_to(key, (8, NPT))
    for a in range(out_ref.shape[0]):
        out_ref[a, 0:8, :] = force
        out_ref[a, 8:16, :] = keys


def window_kernel(place_ref, now_hbm, before_hbm, mod_hbm, xlo_hbm, xhi_hbm, ylo_hbm, yhi_hbm,
                  fl_ref, fc_ref, fr_ref, next_hbm, prior_hbm,
                  a_ref, b_ref, m_ref, kx_ref, ky_ref, kz_ref, kc_ref, d_ref, code_ref, code_smem, list_smem,
                  sems, sem_code, sem_out):
    tiles = fc_ref.shape[0]
    copies = []
    for k, (own, ext) in enumerate(((now_hbm, a_ref), (before_hbm, b_ref), (mod_hbm, m_ref))):
        pieces = (
            (own, ext.at[pl.ds(H, CX), pl.ds(2 * H, CY)]),
            (xlo_hbm.at[pl.ds(k * H, H)], ext.at[pl.ds(0, H), pl.ds(2 * H, CY)]),
            (xhi_hbm.at[pl.ds(k * H, H)], ext.at[pl.ds(H + CX, H), pl.ds(2 * H, CY)]),
            (ylo_hbm.at[pl.ds(k * EX, EX)], ext.at[:, pl.ds(H, H)]),
            (yhi_hbm.at[pl.ds(k * EX, EX)], ext.at[:, pl.ds(2 * H + CY, H)]),
        )
        for n, (src, dst) in enumerate(pieces):
            copies.append(pltpu.make_async_copy(src, dst, sems.at[k, n]))
    for c in copies:
        c.start()

    my_y = place_ref[0]
    lane = lax.broadcasted_iota(jnp.int32, (tiles, NPT), 1)
    part = lax.broadcasted_iota(jnp.int32, (tiles, NPT), 0)
    for side, f_ref in enumerate((fl_ref, fc_ref, fr_ref)):
        key = f_ref[:, 8, :].astype(jnp.int32) - 1
        own = key >> 17
        cell = key & (CELLS - 1)
        gx = (cell >> 12) + (side - 1) * CX + H
        gy = (own - my_y) * CY + ((cell >> 7) & (CY - 1)) + H
        inside = (key >= 0) & (gx >= 1) & (gx < EX - 1) & (gy >= 1) & (gy < EY - 1)
        row = gx * EY + gy
        place = (side * tiles + part) * NPT + lane
        packed = (row << (Z_BITS + P_BITS)) | ((cell & (CZ - 1)) << P_BITS) | place
        code_ref[pl.ds(side * tiles, tiles), :] = jnp.where(inside, packed, -1)
    code_copy = pltpu.make_async_copy(code_ref, code_smem, sem_code)
    code_copy.start()

    def clear(i, _):
        base = pl.multiple_of(i * 64, 64)
        for j in range(8):
            d_ref[pl.ds(base + 8 * j, 8), :] = jnp.zeros((8, CZ), jnp.float32)
        return 0

    lax.fori_loop(0, ROWS * STEPS // 64, clear, 0)
    code_copy.wait()

    def pick_row(r, count):
        for c in range(NPT):
            code = code_smem[r, c]
            list_smem[count] = code
            count = count + jnp.where(code >= 0, 1, 0)
        return count

    count = lax.fori_loop(0, 3 * tiles, pick_row, 0)
    for j in range(4):
        list_smem[count + j] = 0

    zline = lax.broadcasted_iota(jnp.int32, (STEPS, CZ), 1)

    def put(f_ref, tile, code):
        place = code & ((1 << P_BITS) - 1)
        z = (code >> P_BITS) & (CZ - 1)
        row = code >> (Z_BITS + P_BITS)
        force = f_ref[tile, 0:8, :]
        column = jnp.take_along_axis(force, jnp.full((STEPS, CZ), place & (NPT - 1), jnp.int32), axis=1)
        at = pl.ds(pl.multiple_of(row * STEPS, STEPS), STEPS)
        d_ref[at, :] = d_ref[at, :] + jnp.where(zline == z, column, 0.0)

    def add_point(i, _):
        for j in range(4):
            code = list_smem[4 * i + j]
            tile = (code & ((1 << P_BITS) - 1)) >> 7
            put(f_all, tile, code)
        return 0

    f_all = kc_ref
    for side, f_ref in enumerate((fl_ref, fc_ref, fr_ref)):
        for a in range(tiles):
            kc_ref[side * tiles + a, 0:8, :] = f_ref[a, 0:8, :]
    lax.fori_loop(0, (count + 3) // 4, add_point, 0)

    for c in copies:
        c.wait()

    zpos = lax.broadcasted_iota(jnp.int32, (8, CZ), 1)

    def face(c, n):
        return jnp.where(jnp.minimum(c, n) > 0.0, 0.075 * (c + n), 0.0)

    def coefficients(x, _):
        for j in range(EY // 8):
            y = H + 8 * j
            c = m_ref[x, pl.ds(y, 8), :]
            xp = m_ref[x + 1, pl.ds(y, 8), :]
            xm = m_ref[jnp.maximum(x - 1, 0), pl.ds(y, 8), :]
            yp = m_ref[x, pl.ds(y + 1, 8), :]
            ym = m_ref[x, pl.ds(y - 1, 8), :]
            zp = jnp.where(zpos == CZ - 1, 0.0, pltpu.roll(c, CZ - 1, 1))
            zm = jnp.where(zpos == 0, 0.0, pltpu.roll(c, 1, 1))
            kx_ref[x, pl.ds(y, 8), :] = face(c, xp)
            ky_ref[x, pl.ds(y, 8), :] = face(c, yp)
            kz_ref[x, pl.ds(y, 8), :] = face(c, zp)
            kc_ref[x, pl.ds(y, 8), :] = 2.0 - 0.075 * (6.0 * c + ((xp + xm) + (yp + ym) + (zp + zm)))
        return 0

    lax.fori_loop(0, EX - 1, coefficients, 0)

    for step in range(STEPS):
        u_ref, w_ref = (a_ref, b_ref) if step % 2 == 0 else (b_ref, a_ref)

        def advance(x, _, u_ref=u_ref, w_ref=w_ref, step=step):
            for j in range(EY // 8):
                y = H + 8 * j
                u = u_ref[x, pl.ds(y, 8), :]
                kz = kz_ref[x, pl.ds(y, 8), :]
                in_x = (kx_ref[x, pl.ds(y, 8), :] * u_ref[x + 1, pl.ds(y, 8), :]
                        + kx_ref[x - 1, pl.ds(y, 8), :] * u_ref[x - 1, pl.ds(y, 8), :])
                in_y = (ky_ref[x, pl.ds(y, 8), :] * u_ref[x, pl.ds(y + 1, 8), :]
                        + ky_ref[x, pl.ds(y - 1, 8), :] * u_ref[x, pl.ds(y - 1, 8), :])
                in_z = kz * pltpu.roll(u, CZ - 1, 1) + pltpu.roll(kz * u, 1, 1)
                drive = d_ref[pl.ds((x * EY + 8 * j) * STEPS + step, 8, stride=STEPS), :]
                own = kc_ref[x, pl.ds(y, 8), :] * u - w_ref[x, pl.ds(y, 8), :]
                w_ref[x, pl.ds(y, 8), :] = (own + drive) + ((in_x + in_y) + in_z)
            return 0

        lax.fori_loop(step + 1, EX - step - 1, advance, 0)

    outs = [
        pltpu.make_async_copy(ref.at[pl.ds(H, CX), pl.ds(2 * H, CY)], hbm, sem_out.at[n])
        for n, (ref, hbm) in enumerate(((a_ref, next_hbm), (b_ref, prior_hbm)))
    ]
    for c in outs:
        c.start()
    for c in outs:
        c.wait()


def window(place, fields, forces):
    tiles = forces[0].shape[0]
    grid = jax.ShapeDtypeStruct((CX, CY, CZ), jnp.float32)
    buffer = pltpu.VMEM((EX, PY, CZ), jnp.float32)
    return pl.pallas_call(
        window_kernel,
        out_shape=(grid, grid),
        in_specs=[pl.BlockSpec(memory_space=pltpu.SMEM)] + [any_spec()] * 7 + [vmem_spec()] * 3,
        out_specs=(any_spec(), any_spec()),
        scratch_shapes=[buffer] * 7 + [
            pltpu.VMEM((ROWS * STEPS, CZ), jnp.float32),
            pltpu.VMEM((3 * tiles, NPT), jnp.int32),
            pltpu.SMEM((3 * tiles, NPT), jnp.int32),
            pltpu.SMEM((3 * tiles * NPT + 8,), jnp.int32),
            pltpu.SemaphoreType.DMA((3, 5)),
            pltpu.SemaphoreType.DMA,
            pltpu.SemaphoreType.DMA((2,)),
        ],
        compiler_params=pltpu.CompilerParams(vmem_limit_bytes=LIMIT),
    )(place, *fields, *forces)


def neighbours(low, high, axis):
    count = lax.axis_size(axis)
    up = [(i, i + 1) for i in range(count - 1)]
    down = [(i + 1, i) for i in range(count - 1)]
    return lax.ppermute(high, axis, up), lax.ppermute(low, axis, down)


def shards(field_now, field_before, layer, modulus_table, fk_panel, owner, local_cell):
    sources, tiles = lax.axis_size("along"), lax.axis_size("across")
    local_freqs = fk_panel.shape[1]
    modulus = jnp.zeros(field_now.shape, jnp.float32)
    for level in range(modulus_table.shape[0]):
        modulus = modulus + jnp.where(layer == level, modulus_table[level], 0.0)
    arrays = (field_now, field_before, modulus)

    dealt = pl.pallas_call(
        deal_kernel,
        out_shape=jax.ShapeDtypeStruct((sources, 2 * local_freqs, NPT), jnp.bfloat16),
        in_specs=[vmem_spec()],
        out_specs=vmem_spec(),
    )(fk_panel.reshape(2, local_freqs, sources * NPT))

    xlo, xhi = neighbours(
        jnp.concatenate([a[:H] for a in arrays], axis=0),
        jnp.concatenate([a[-H:] for a in arrays], axis=0),
        "along",
    )
    moved = lax.all_to_all(dealt, "along", 0, 0, tiled=True)

    def side(rows):
        return jnp.concatenate(
            [p[:, rows] for k, a in enumerate(arrays) for p in (xlo[k * H:k * H + H], a, xhi[k * H:k * H + H])],
            axis=0,
        )

    ylo, yhi = neighbours(side(slice(0, H)), side(slice(CY - H, CY)), "across")

    payload = pl.pallas_call(
        transform_kernel,
        out_shape=jax.ShapeDtypeStruct((tiles, 16, NPT), jnp.float32),
        in_specs=[vmem_spec()] * 4,
        out_specs=vmem_spec(),
        scratch_shapes=[pltpu.VMEM((2 * local_freqs * sources, NPT), jnp.float32)],
    )(moved, jnp.asarray(split_table(sources, local_freqs)), owner.reshape(1, NPT), local_cell)
    center = lax.all_to_all(payload, "across", 0, 0, tiled=True)
    left, right = neighbours(center, center, "along")
    place = lax.axis_index("across").astype(jnp.int32).reshape(1)
    return window(place, (*arrays, xlo, xhi, ylo, yhi), (left, center, right))


def solution(mesh):
    placed = (
        P("along", "across", None),
        P("along", "across", None),
        P("along", "across", None),
        P(),
        P(None, "along", "across", None),
        P("across", "along", None),
        P("across", "along"),
    )
    return jax.shard_map(
        shards,
        mesh=mesh,
        in_specs=placed,
        out_specs=(P("along", "across", None), P("along", "across", None)),
        check_vma=False,
    )
```

```python
import math

import jax
import jax.numpy as jnp
import ml_dtypes
import numpy as np
from jax import lax
from jax.experimental import pallas as pl
from jax.experimental.pallas import tpu as pltpu
from jax.sharding import PartitionSpec as P

STEPS = 8
H = 8
CX, CY, CZ = 32, 32, 128
EX, EY = CX + 2 * H, CY + 2 * H
PY = EY + 2 * H
ROWS = EX * EY
CELLS = CX * CY * CZ
NPT = 128
ROW_BITS, Z_BITS, P_BITS = 12, 7, 12
BODY = (12, 11, 11, 10, 10, 9, 9, 8)
GROUP = 16
LIMIT = 56 * 1024 * 1024


def vmem_spec():
    return pl.BlockSpec(memory_space=pltpu.VMEM)


def any_spec():
    return pl.BlockSpec(memory_space=pl.ANY)


def split_table(sources, local_freqs):
    total = sources * local_freqs
    freq = np.arange(total, dtype=np.float64).reshape(sources, 1, local_freqs)
    times = np.arange(STEPS, dtype=np.float64).reshape(STEPS, 1, 1, 1)
    phase = math.pi * times * freq[None] / total
    table = np.concatenate([np.cos(phase), -np.sin(phase)], axis=2) / math.sqrt(total)
    rest = table.reshape(STEPS, 2 * total).astype(np.float32)
    parts = []
    for _ in range(3):
        part = rest.astype(ml_dtypes.bfloat16)
        parts.append(part)
        rest = rest - part.astype(np.float32)
    return np.concatenate(parts, axis=0)


def prepare_kernel(table_ref, now_ref, before_ref, layer_ref, fk_ref, low_ref, high_ref, dealt_ref, mod_ref):
    for i in range(dealt_ref.shape[0]):
        for c in range(2):
            dealt_ref[i, pl.ds(2 * c, 2), :] = fk_ref[c, :, pl.ds(i * NPT, NPT)]

    def fill(x, _):
        level = layer_ref[x]
        modulus = jnp.full(level.shape, table_ref[0], jnp.float32)
        for k in range(1, table_ref.shape[0]):
            modulus = jnp.where(level == k, table_ref[k], modulus)
        mod_ref[x] = modulus
        return 0

    lax.fori_loop(0, CX, fill, 0, unroll=2)
    for k, ref in enumerate((now_ref, before_ref, mod_ref)):
        low_ref[pl.ds(k * H, H)] = ref[pl.ds(0, H)]
        high_ref[pl.ds(k * H, H)] = ref[pl.ds(CX - H, H)]


def transform_kernel(moved_ref, table_ref, owner_ref, cell_ref, out_ref, wide_ref):
    for i in range(moved_ref.shape[0]):
        wide_ref[pl.ds(4 * i, 4), :] = moved_ref[i].astype(jnp.float32)
    panel = wide_ref[...].astype(jnp.bfloat16)
    parts = jnp.dot(table_ref[...], panel, preferred_element_type=jnp.float32)
    force = parts[0:8] + parts[8:16] + parts[16:24]
    key = (owner_ref[...] * CELLS + cell_ref[...] + 1).astype(jnp.float32)
    keys = jnp.broadcast_to(key, (8, NPT))
    for a in range(out_ref.shape[0]):
        out_ref[a, 0:8, :] = force
        out_ref[a, 8:16, :] = keys


def window_kernel(place_ref, now_hbm, before_hbm, mod_hbm, xlo_hbm, xhi_hbm, ylo_hbm, yhi_hbm,
                  fl_ref, fc_ref, fr_ref, next_hbm, prior_hbm,
                  a_ref, b_ref, m_ref, kx_ref, ky_ref, kz_ref, kc_ref, d_ref, code_ref, code_smem, list_smem,
                  sems, sem_code, sem_out):
    tiles = fc_ref.shape[0]
    copies = []
    for k, (own, ext) in enumerate(((now_hbm, a_ref), (before_hbm, b_ref), (mod_hbm, m_ref))):
        pieces = (
            (own, ext.at[pl.ds(1 + H, CX), pl.ds(2 * H, CY)]),
            (xlo_hbm.at[pl.ds(k * H, H)], ext.at[pl.ds(1, H), pl.ds(2 * H, CY)]),
            (xhi_hbm.at[pl.ds(k * H, H)], ext.at[pl.ds(1 + H + CX, H), pl.ds(2 * H, CY)]),
            (ylo_hbm.at[pl.ds(k * EX, EX)], ext.at[pl.ds(1, EX), pl.ds(H, H)]),
            (yhi_hbm.at[pl.ds(k * EX, EX)], ext.at[pl.ds(1, EX), pl.ds(2 * H + CY, H)]),
        )
        for n, (src, dst) in enumerate(pieces):
            copies.append(pltpu.make_async_copy(src, dst, sems.at[k, n]))
    for c in copies:
        c.start()

    my_y = place_ref[0]
    lane = lax.broadcasted_iota(jnp.int32, (tiles, NPT), 1)
    part = lax.broadcasted_iota(jnp.int32, (tiles, NPT), 0)
    for side, f_ref in enumerate((fl_ref, fc_ref, fr_ref)):
        key = f_ref[:, 8, :].astype(jnp.int32) - 1
        own = key >> 17
        cell = key & (CELLS - 1)
        gx = (cell >> 12) + (side - 1) * CX + H
        gy = (own - my_y) * CY + ((cell >> 7) & (CY - 1)) + H
        inside = (key >= 0) & (gx >= 1) & (gx < EX - 1) & (gy >= 1) & (gy < EY - 1)
        row = gx * EY + gy
        place = (side * tiles + part) * NPT + lane
        packed = (row << (Z_BITS + P_BITS)) | ((cell & (CZ - 1)) << P_BITS) | place
        code_ref[pl.ds(side * tiles, tiles), :] = jnp.where(inside, packed, -1)
    code_copy = pltpu.make_async_copy(code_ref, code_smem, sem_code)
    code_copy.start()

    def clear(i, _):
        base = pl.multiple_of(i * 64, 64)
        for j in range(8):
            d_ref[pl.ds(base + 8 * j, 8), :] = jnp.zeros((8, CZ), jnp.float32)
        return 0

    lax.fori_loop(0, ROWS * STEPS // 64, clear, 0)
    code_copy.wait()

    def pick_row(r, count):
        for c in range(NPT):
            code = code_smem[r, c]
            list_smem[count] = code
            count = count + jnp.where(code >= 0, 1, 0)
        return count

    count = lax.fori_loop(0, 3 * tiles, pick_row, 0)
    for j in range(GROUP):
        list_smem[count + j] = 0

    zline = lax.broadcasted_iota(jnp.int32, (STEPS, CZ), 1)

    def add_points(i, _):
        adds = []
        for j in range(GROUP):
            code = list_smem[GROUP * i + j]
            place = code & ((1 << P_BITS) - 1)
            z = (code >> P_BITS) & (CZ - 1)
            row = code >> (Z_BITS + P_BITS)
            force = f_all[place >> 7, 0:8, :]
            column = jnp.take_along_axis(force, jnp.full((STEPS, CZ), place & (NPT - 1), jnp.int32), axis=1)
            adds.append((pl.ds(pl.multiple_of(row * STEPS, STEPS), STEPS), jnp.where(zline == z, column, 0.0)))
        for at, add in adds:
            d_ref[at, :] = d_ref[at, :] + add
        return 0

    f_all = kc_ref
    for side, f_ref in enumerate((fl_ref, fc_ref, fr_ref)):
        for a in range(tiles):
            kc_ref[side * tiles + a, 0:8, :] = f_ref[a, 0:8, :]
    lax.fori_loop(0, (count + GROUP - 1) // GROUP, add_points, 0)

    for c in copies:
        c.wait()

    zpos = lax.broadcasted_iota(jnp.int32, (8, CZ), 1)

    def face(c, n):
        return jnp.where(jnp.minimum(c, n) > 0.0, 0.075 * (c + n), 0.0)

    def coefficients(i, _):
        for k in range(8):
            x = 8 * i + k + 1
            for j in range(EY // 8):
                y = H + 8 * j
                c = m_ref[x, pl.ds(y, 8), :]
                xp = m_ref[x + 1, pl.ds(y, 8), :]
                xm = m_ref[x - 1, pl.ds(y, 8), :]
                yp = m_ref[x, pl.ds(y + 1, 8), :]
                ym = m_ref[x, pl.ds(y - 1, 8), :]
                zp = jnp.where(zpos == CZ - 1, 0.0, pltpu.roll(c, CZ - 1, 1))
                zm = jnp.where(zpos == 0, 0.0, pltpu.roll(c, 1, 1))
                kx_ref[x, pl.ds(y, 8), :] = face(c, xp)
                ky_ref[x, pl.ds(y, 8), :] = face(c, yp)
                kz_ref[x, pl.ds(y, 8), :] = face(c, zp)
                kc_ref[x, pl.ds(y, 8), :] = 2.0 - 0.075 * (6.0 * c + ((xp + xm) + (yp + ym) + (zp + zm)))
        return 0

    lax.fori_loop(0, EX // 8, coefficients, 0)

    for step in range(STEPS):
        u_ref, w_ref = (a_ref, b_ref) if step % 2 == 0 else (b_ref, a_ref)

        planes = BODY[step]
        start = EX // 2 - 2 * planes
        rows = range(0, EY // 8) if step < STEPS - 1 else range(1, 1 + CY // 8)

        def advance(i, _, u_ref=u_ref, w_ref=w_ref, step=step, planes=planes, start=start, rows=rows):
            for k in range(planes):
                x = start + planes * i + k
                for j in rows:
                    y = H + 8 * j
                    u = u_ref[x + 1, pl.ds(y, 8), :]
                    kz = kz_ref[x + 1, pl.ds(y, 8), :]
                    in_z = kz * pltpu.roll(u, CZ - 1, 1) + pltpu.roll(kz * u, 1, 1)
                    in_x = (kx_ref[x + 1, pl.ds(y, 8), :] * u_ref[x + 2, pl.ds(y, 8), :]
                            + kx_ref[x, pl.ds(y, 8), :] * u_ref[x, pl.ds(y, 8), :])
                    in_y = (ky_ref[x + 1, pl.ds(y, 8), :] * u_ref[x + 1, pl.ds(y + 1, 8), :]
                            + ky_ref[x + 1, pl.ds(y - 1, 8), :] * u_ref[x + 1, pl.ds(y - 1, 8), :])
                    drive = d_ref[pl.ds((x * EY + 8 * j) * STEPS + step, 8, stride=STEPS), :]
                    own = kc_ref[x + 1, pl.ds(y, 8), :] * u - w_ref[x + 1, pl.ds(y, 8), :]
                    w_ref[x + 1, pl.ds(y, 8), :] = (own + drive) + ((in_x + in_y) + in_z)
            return 0

        lax.fori_loop(0, 4, advance, 0)

    outs = [
        pltpu.make_async_copy(ref.at[pl.ds(1 + H, CX), pl.ds(2 * H, CY)], hbm, sem_out.at[n])
        for n, (ref, hbm) in enumerate(((a_ref, next_hbm), (b_ref, prior_hbm)))
    ]
    for c in outs:
        c.start()
    for c in outs:
        c.wait()


def window(place, fields, forces):
    tiles = forces[0].shape[0]
    grid = jax.ShapeDtypeStruct((CX, CY, CZ), jnp.float32)
    buffer = pltpu.VMEM((EX + 2, PY, CZ), jnp.float32)
    return pl.pallas_call(
        window_kernel,
        out_shape=(grid, grid),
        in_specs=[pl.BlockSpec(memory_space=pltpu.SMEM)] + [any_spec()] * 7 + [vmem_spec()] * 3,
        out_specs=(any_spec(), any_spec()),
        scratch_shapes=[buffer] * 7 + [
            pltpu.VMEM((ROWS * STEPS, CZ), jnp.float32),
            pltpu.VMEM((3 * tiles, NPT), jnp.int32),
            pltpu.SMEM((3 * tiles, NPT), jnp.int32),
            pltpu.SMEM((3 * tiles * NPT + 8,), jnp.int32),
            pltpu.SemaphoreType.DMA((3, 5)),
            pltpu.SemaphoreType.DMA,
            pltpu.SemaphoreType.DMA((2,)),
        ],
        compiler_params=pltpu.CompilerParams(vmem_limit_bytes=LIMIT),
    )(place, *fields, *forces)


def neighbours(low, high, axis):
    count = lax.axis_size(axis)
    up = [(i, i + 1) for i in range(count - 1)]
    down = [(i + 1, i) for i in range(count - 1)]
    return lax.ppermute(high, axis, up), lax.ppermute(low, axis, down)


def shards(field_now, field_before, layer, modulus_table, fk_panel, owner, local_cell):
    sources, tiles = lax.axis_size("along"), lax.axis_size("across")
    local_freqs = fk_panel.shape[1]
    slab = jax.ShapeDtypeStruct((3 * H, CY, CZ), jnp.float32)
    low, high, dealt, modulus = pl.pallas_call(
        prepare_kernel,
        out_shape=(
            slab,
            slab,
            jax.ShapeDtypeStruct((sources, 2 * local_freqs, NPT), jnp.bfloat16),
            jax.ShapeDtypeStruct(field_now.shape, jnp.float32),
        ),
        in_specs=[pl.BlockSpec(memory_space=pltpu.SMEM)] + [vmem_spec()] * 4,
        out_specs=(vmem_spec(),) * 4,
        compiler_params=pltpu.CompilerParams(vmem_limit_bytes=LIMIT),
    )(modulus_table, field_now, field_before, layer, fk_panel.reshape(2, local_freqs, sources * NPT))
    arrays = (field_now, field_before, modulus)
    xlo, xhi = neighbours(low, high, "along")
    moved = lax.all_to_all(dealt, "along", 0, 0, tiled=True)
    xlo, xhi, moved = lax.optimization_barrier((xlo, xhi, moved))

    def side(rows):
        return jnp.concatenate(
            [p[:, rows] for k, a in enumerate(arrays) for p in (xlo[k * H:k * H + H], a, xhi[k * H:k * H + H])],
            axis=0,
        )

    ylo, yhi = neighbours(side(slice(0, H)), side(slice(CY - H, CY)), "across")

    payload = pl.pallas_call(
        transform_kernel,
        out_shape=jax.ShapeDtypeStruct((tiles, 16, NPT), jnp.float32),
        in_specs=[vmem_spec()] * 4,
        out_specs=vmem_spec(),
        scratch_shapes=[pltpu.VMEM((2 * local_freqs * sources, NPT), jnp.float32)],
    )(moved, jnp.asarray(split_table(sources, local_freqs)), owner.reshape(1, NPT), local_cell)
    center = lax.all_to_all(payload, "across", 0, 0, tiled=True)
    left, right = neighbours(center, center, "along")
    place = lax.axis_index("across").astype(jnp.int32).reshape(1)
    return window(place, (*arrays, xlo, xhi, ylo, yhi), (left, center, right))


def solution(mesh):
    placed = (
        P("along", "across", None),
        P("along", "across", None),
        P("along", "across", None),
        P(),
        P(None, "along", "across", None),
        P("across", "along", None),
        P("across", "along"),
    )
    return jax.shard_map(
        shards,
        mesh=mesh,
        in_specs=placed,
        out_specs=(P("along", "across", None), P("along", "across", None)),
        check_vma=False,
    )
```

```python
import math

import jax
import jax.numpy as jnp
import ml_dtypes
import numpy as np
from jax import lax
from jax.experimental import pallas as pl
from jax.experimental.pallas import tpu as pltpu
from jax.sharding import PartitionSpec as P

STEPS = 8
H = 8
CX, CY, CZ = 32, 32, 128
EX, EY = CX + 2 * H, CY + 2 * H
PY = EY + 2 * H
ROWS = EX * EY
CELLS = CX * CY * CZ
NPT = 128
ROW_BITS, Z_BITS, P_BITS = 12, 7, 12
BODY = (12, 11, 11, 10, 10, 9, 9, 8)
GROUP = 16
LIMIT = 28 * 1024 * 1024


def vmem_spec():
    return pl.BlockSpec(memory_space=pltpu.VMEM)


def any_spec():
    return pl.BlockSpec(memory_space=pl.ANY)


def split_table(sources, local_freqs):
    total = sources * local_freqs
    freq = np.arange(total, dtype=np.float64).reshape(sources, 1, local_freqs)
    times = np.arange(STEPS, dtype=np.float64).reshape(STEPS, 1, 1, 1)
    phase = math.pi * times * freq[None] / total
    table = np.concatenate([np.cos(phase), -np.sin(phase)], axis=2) / math.sqrt(total)
    rest = table.reshape(STEPS, 2 * total).astype(np.float32)
    parts = []
    for _ in range(3):
        part = rest.astype(ml_dtypes.bfloat16)
        parts.append(part)
        rest = rest - part.astype(np.float32)
    return np.concatenate(parts, axis=0)


def prepare_kernel(table_ref, now_ref, before_ref, layer_ref, fk_ref, low_ref, high_ref, dealt_ref, mod_ref):
    for i in range(dealt_ref.shape[0]):
        for c in range(2):
            dealt_ref[i, pl.ds(2 * c, 2), :] = fk_ref[c, :, pl.ds(i * NPT, NPT)]

    def fill(x, _):
        level = layer_ref[x]
        modulus = jnp.full(level.shape, table_ref[0], jnp.float32)
        for k in range(1, table_ref.shape[0]):
            modulus = jnp.where(level == k, table_ref[k], modulus)
        mod_ref[x] = modulus
        return 0

    lax.fori_loop(0, CX, fill, 0, unroll=2)
    for k, ref in enumerate((now_ref, before_ref, mod_ref)):
        low_ref[pl.ds(k * CX, CX)] = ref[:, pl.ds(0, H), :]
        high_ref[pl.ds(k * CX, CX)] = ref[:, pl.ds(CY - H, H), :]


def middle_kernel(moved_ref, table_ref, owner_ref, cell_ref, now_hbm, before_hbm, mod_hbm, ylo_hbm, yhi_hbm,
                  out_ref, low_hbm, high_hbm, wide_ref, sems):
    copies = []
    for k, own in enumerate((now_hbm, before_hbm, mod_hbm)):
        for n, (slab, x) in enumerate(((low_hbm, 0), (high_hbm, CX - H))):
            rows = slab.at[pl.ds(k * H, H)]
            for m, (src, y, wide) in enumerate((
                (ylo_hbm.at[pl.ds(k * CX + x, H)], 0, H),
                (own.at[pl.ds(x, H)], H, CY),
                (yhi_hbm.at[pl.ds(k * CX + x, H)], H + CY, H),
            )):
                copies.append(pltpu.make_async_copy(src, rows.at[:, pl.ds(y, wide)], sems.at[k, n, m]))
    for c in copies:
        c.start()
    for i in range(moved_ref.shape[0]):
        wide_ref[pl.ds(4 * i, 4), :] = moved_ref[i].astype(jnp.float32)
    panel = wide_ref[...].astype(jnp.bfloat16)
    parts = jnp.dot(table_ref[...], panel, preferred_element_type=jnp.float32)
    force = parts[0:8] + parts[8:16] + parts[16:24]
    key = (owner_ref[...] * CELLS + cell_ref[...] + 1).astype(jnp.float32)
    keys = jnp.broadcast_to(key, (8, NPT))
    for a in range(out_ref.shape[0]):
        out_ref[a, 0:8, :] = force
        out_ref[a, 8:16, :] = keys
    for c in copies:
        c.wait()


def window_kernel(place_ref, now_hbm, before_hbm, mod_hbm, ylo_hbm, yhi_hbm, xlo_hbm, xhi_hbm,
                  fl_ref, fc_ref, fr_ref, next_hbm, prior_hbm,
                  a_ref, b_ref, m_ref, kx_ref, ky_ref, kz_ref, kc_ref, d_ref, code_ref, rank_ref, code_smem, rank_smem, list_smem,
                  sems, sem_code, sem_out):
    tiles = fc_ref.shape[0]
    copies = []
    for k, (own, ext) in enumerate(((now_hbm, a_ref), (before_hbm, b_ref), (mod_hbm, m_ref))):
        pieces = (
            (own, ext.at[pl.ds(1 + H, CX), pl.ds(2 * H, CY)]),
            (ylo_hbm.at[pl.ds(k * CX, CX)], ext.at[pl.ds(1 + H, CX), pl.ds(H, H)]),
            (yhi_hbm.at[pl.ds(k * CX, CX)], ext.at[pl.ds(1 + H, CX), pl.ds(2 * H + CY, H)]),
            (xlo_hbm.at[pl.ds(k * H, H)], ext.at[pl.ds(1, H), pl.ds(H, EY)]),
            (xhi_hbm.at[pl.ds(k * H, H)], ext.at[pl.ds(1 + H + CX, H), pl.ds(H, EY)]),
        )
        for n, (src, dst) in enumerate(pieces):
            copies.append(pltpu.make_async_copy(src, dst, sems.at[k, n]))
    for c in copies:
        c.start()

    my_y = place_ref[0]
    lane = lax.broadcasted_iota(jnp.int32, (tiles, NPT), 1)
    part = lax.broadcasted_iota(jnp.int32, (tiles, NPT), 0)
    for side, f_ref in enumerate((fl_ref, fc_ref, fr_ref)):
        key = f_ref[:, 8, :].astype(jnp.int32) - 1
        own = key >> 17
        cell = key & (CELLS - 1)
        gx = (cell >> 12) + (side - 1) * CX + H
        gy = (own - my_y) * CY + ((cell >> 7) & (CY - 1)) + H
        inside = (key >= 0) & (gx >= 1) & (gx < EX - 1) & (gy >= 1) & (gy < EY - 1)
        row = gx * EY + gy
        place = (side * tiles + part) * NPT + lane
        packed = (row << (Z_BITS + P_BITS)) | ((cell & (CZ - 1)) << P_BITS) | place
        code_ref[pl.ds(side * tiles, tiles), :] = jnp.where(inside, packed, -1)
    code = code_ref[...]
    found = jnp.where(code >= 0, 1.0, 0.0)
    ahead = jnp.where(
        lax.broadcasted_iota(jnp.int32, (NPT, NPT), 0) < lax.broadcasted_iota(jnp.int32, (NPT, NPT), 1), 1.0, 0.0)
    in_row = jnp.dot(found.astype(jnp.bfloat16), ahead.astype(jnp.bfloat16), preferred_element_type=jnp.float32)
    below = jnp.where(
        lax.broadcasted_iota(jnp.int32, (4 * tiles, 3 * tiles), 0) > lax.broadcasted_iota(jnp.int32, (4 * tiles, 3 * tiles), 1),
        1.0, 0.0)
    rows_before = jnp.dot(below.astype(jnp.bfloat16), found.astype(jnp.bfloat16), preferred_element_type=jnp.float32)
    before = jnp.sum(rows_before, axis=1, keepdims=True)
    rank_ref[pl.ds(0, 3 * tiles), :] = jnp.where(
        code >= 0, in_row + before[0:3 * tiles], 3.0 * tiles * NPT + GROUP).astype(jnp.int32)
    rank_ref[pl.ds(3 * tiles, tiles), :] = jnp.broadcast_to(before[3 * tiles:4 * tiles], (tiles, NPT)).astype(jnp.int32)
    code_copies = (
        pltpu.make_async_copy(code_ref, code_smem, sem_code.at[0]),
        pltpu.make_async_copy(rank_ref, rank_smem, sem_code.at[1]),
    )
    for c in code_copies:
        c.start()

    def clear(i, _):
        base = pl.multiple_of(i * 64, 64)
        for j in range(8):
            d_ref[pl.ds(base + 8 * j, 8), :] = jnp.zeros((8, CZ), jnp.float32)
        return 0

    lax.fori_loop(0, ROWS * STEPS // 64, clear, 0)
    for c in code_copies:
        c.wait()

    def pick_row(r, _):
        for c in range(NPT):
            list_smem[rank_smem[r, c]] = code_smem[r, c]
        return 0

    lax.fori_loop(0, 3 * tiles, pick_row, 0)
    count = rank_smem[3 * tiles, 0]
    for j in range(GROUP):
        list_smem[count + j] = 0

    zline = lax.broadcasted_iota(jnp.int32, (STEPS, CZ), 1)

    def add_points(i, _):
        adds = []
        for j in range(GROUP):
            code = list_smem[GROUP * i + j]
            place = code & ((1 << P_BITS) - 1)
            z = (code >> P_BITS) & (CZ - 1)
            row = code >> (Z_BITS + P_BITS)
            force = f_all[place >> 7, 0:8, :]
            column = jnp.take_along_axis(force, jnp.full((STEPS, CZ), place & (NPT - 1), jnp.int32), axis=1)
            adds.append((pl.ds(pl.multiple_of(row * STEPS, STEPS), STEPS), jnp.where(zline == z, column, 0.0)))
        for at, add in adds:
            d_ref[at, :] = d_ref[at, :] + add
        return 0

    f_all = kc_ref
    for side, f_ref in enumerate((fl_ref, fc_ref, fr_ref)):
        for a in range(tiles):
            kc_ref[side * tiles + a, 0:8, :] = f_ref[a, 0:8, :]
    lax.fori_loop(0, (count + GROUP - 1) // GROUP, add_points, 0)

    for c in copies:
        c.wait()

    zpos = lax.broadcasted_iota(jnp.int32, (8, CZ), 1)

    def face(c, n):
        return jnp.where(jnp.minimum(c, n) > 0.0, 0.075 * (c + n), 0.0)

    def coefficients(i, _):
        for k in range(8):
            x = 8 * i + k + 1
            for j in range(EY // 8):
                y = H + 8 * j
                c = m_ref[x, pl.ds(y, 8), :]
                xp = m_ref[x + 1, pl.ds(y, 8), :]
                xm = m_ref[x - 1, pl.ds(y, 8), :]
                yp = m_ref[x, pl.ds(y + 1, 8), :]
                ym = m_ref[x, pl.ds(y - 1, 8), :]
                zp = jnp.where(zpos == CZ - 1, 0.0, pltpu.roll(c, CZ - 1, 1))
                zm = jnp.where(zpos == 0, 0.0, pltpu.roll(c, 1, 1))
                kx_ref[x, pl.ds(y, 8), :] = face(c, xp)
                ky_ref[x, pl.ds(y, 8), :] = face(c, yp)
                kz_ref[x, pl.ds(y, 8), :] = face(c, zp)
                kc_ref[x, pl.ds(y, 8), :] = 2.0 - 0.075 * (6.0 * c + ((xp + xm) + (yp + ym) + (zp + zm)))
        return 0

    lax.fori_loop(0, EX // 8, coefficients, 0)

    next_copy, prior_copy = (
        pltpu.make_async_copy(ref.at[pl.ds(1 + H, CX), pl.ds(2 * H, CY)], hbm, sem_out.at[n])
        for n, (ref, hbm) in enumerate(((a_ref, next_hbm), (b_ref, prior_hbm)))
    )
    for step in range(STEPS):
        u_ref, w_ref = (a_ref, b_ref) if step % 2 == 0 else (b_ref, a_ref)

        planes = BODY[step]
        start = EX // 2 - 2 * planes
        rows = range(0, EY // 8) if step < STEPS - 1 else range(1, 1 + CY // 8)

        def advance(i, _, u_ref=u_ref, w_ref=w_ref, step=step, planes=planes, start=start, rows=rows):
            for k in range(planes):
                x = start + planes * i + k
                for j in rows:
                    y = H + 8 * j
                    u = u_ref[x + 1, pl.ds(y, 8), :]
                    kz = kz_ref[x + 1, pl.ds(y, 8), :]
                    in_z = kz * pltpu.roll(u, CZ - 1, 1) + pltpu.roll(kz * u, 1, 1)
                    in_x = (kx_ref[x + 1, pl.ds(y, 8), :] * u_ref[x + 2, pl.ds(y, 8), :]
                            + kx_ref[x, pl.ds(y, 8), :] * u_ref[x, pl.ds(y, 8), :])
                    in_y = (ky_ref[x + 1, pl.ds(y, 8), :] * u_ref[x + 1, pl.ds(y + 1, 8), :]
                            + ky_ref[x + 1, pl.ds(y - 1, 8), :] * u_ref[x + 1, pl.ds(y - 1, 8), :])
                    drive = d_ref[pl.ds((x * EY + 8 * j) * STEPS + step, 8, stride=STEPS), :]
                    own = kc_ref[x + 1, pl.ds(y, 8), :] * u - w_ref[x + 1, pl.ds(y, 8), :]
                    w_ref[x + 1, pl.ds(y, 8), :] = (own + drive) + ((in_x + in_y) + in_z)
            return 0

        lax.fori_loop(0, 4, advance, 0)

        if step == STEPS - 2:
            prior_copy.start()
    next_copy.start()
    next_copy.wait()
    prior_copy.wait()


def window(place, fields, forces):
    tiles = forces[0].shape[0]
    grid = jax.ShapeDtypeStruct((CX, CY, CZ), jnp.float32)
    buffer = pltpu.VMEM((EX + 2, PY, CZ), jnp.float32)
    return pl.pallas_call(
        window_kernel,
        out_shape=(grid, grid),
        in_specs=[pl.BlockSpec(memory_space=pltpu.SMEM)] + [any_spec()] * 7 + [vmem_spec()] * 3,
        out_specs=(any_spec(), any_spec()),
        scratch_shapes=[buffer] * 7 + [
            pltpu.VMEM((ROWS * STEPS, CZ), jnp.float32),
            pltpu.VMEM((3 * tiles, NPT), jnp.int32),
            pltpu.VMEM((4 * tiles, NPT), jnp.int32),
            pltpu.SMEM((3 * tiles, NPT), jnp.int32),
            pltpu.SMEM((4 * tiles, NPT), jnp.int32),
            pltpu.SMEM((3 * tiles * NPT + 2 * GROUP,), jnp.int32),
            pltpu.SemaphoreType.DMA((3, 5)),
            pltpu.SemaphoreType.DMA((2,)),
            pltpu.SemaphoreType.DMA((2,)),
        ],
        compiler_params=pltpu.CompilerParams(vmem_limit_bytes=LIMIT),
    )(place, *fields, *forces)


def neighbours(low, high, axis):
    count = lax.axis_size(axis)
    up = [(i, i + 1) for i in range(count - 1)]
    down = [(i + 1, i) for i in range(count - 1)]
    return lax.ppermute(high, axis, up), lax.ppermute(low, axis, down)


def shards(field_now, field_before, layer, modulus_table, fk_panel, owner, local_cell):
    sources, tiles = lax.axis_size("along"), lax.axis_size("across")
    local_freqs = fk_panel.shape[1]
    slab = jax.ShapeDtypeStruct((3 * CX, H, CZ), jnp.float32)
    low, high, dealt, modulus = pl.pallas_call(
        prepare_kernel,
        out_shape=(
            slab,
            slab,
            jax.ShapeDtypeStruct((sources, 2 * local_freqs, NPT), jnp.bfloat16),
            jax.ShapeDtypeStruct(field_now.shape, jnp.float32),
        ),
        in_specs=[pl.BlockSpec(memory_space=pltpu.SMEM)] + [vmem_spec()] * 4,
        out_specs=(vmem_spec(),) * 4,
        compiler_params=pltpu.CompilerParams(vmem_limit_bytes=LIMIT),
    )(modulus_table, field_now, field_before, layer, fk_panel.reshape(2, local_freqs, sources * NPT))
    arrays = (field_now, field_before, modulus)
    ylo, yhi = neighbours(low, high, "across")
    moved = lax.all_to_all(dealt, "along", 0, 0, tiled=True)
    ylo, yhi, moved = lax.optimization_barrier((ylo, yhi, moved))

    slab = jax.ShapeDtypeStruct((3 * H, EY, CZ), jnp.float32)
    payload, low, high = pl.pallas_call(
        middle_kernel,
        out_shape=(jax.ShapeDtypeStruct((tiles, 16, NPT), jnp.float32), slab, slab),
        in_specs=[vmem_spec()] * 4 + [any_spec()] * 5,
        out_specs=(vmem_spec(), any_spec(), any_spec()),
        scratch_shapes=[
            pltpu.VMEM((2 * local_freqs * sources, NPT), jnp.float32),
            pltpu.SemaphoreType.DMA((3, 2, 3)),
        ],
    )(moved, jnp.asarray(split_table(sources, local_freqs)), owner.reshape(1, NPT), local_cell, *arrays, ylo, yhi)
    xlo, xhi = neighbours(low, high, "along")
    center = lax.all_to_all(payload, "across", 0, 0, tiled=True)
    left, right = neighbours(center, center, "along")
    place = lax.axis_index("across").astype(jnp.int32).reshape(1)
    return window(place, (*arrays, ylo, yhi, xlo, xhi), (left, center, right))


def solution(mesh):
    placed = (
        P("along", "across", None),
        P("along", "across", None),
        P("along", "across", None),
        P(),
        P(None, "along", "across", None),
        P("across", "along", None),
        P("across", "along"),
    )
    return jax.shard_map(
        shards,
        mesh=mesh,
        in_specs=placed,
        out_specs=(P("along", "across", None), P("along", "across", None)),
        check_vma=False,
    )
```

```python
import math

import jax
import jax.numpy as jnp
import ml_dtypes
import numpy as np
from jax import lax
from jax.experimental import pallas as pl
from jax.experimental.pallas import tpu as pltpu
from jax.sharding import PartitionSpec as P

STEPS = 8
H = 8
CX, CY, CZ = 32, 32, 128
EX, EY = CX + 2 * H, CY + 2 * H
PY = EY + 2 * H
ROWS = EX * EY
CELLS = CX * CY * CZ
NPT = 128
ROW_BITS, Z_BITS, P_BITS = 12, 7, 12
BODY = (12, 11, 11, 10, 10, 9, 9, 8)
GROUP = 16
LIMIT = 58 * 1024 * 1024


def vmem_spec():
    return pl.BlockSpec(memory_space=pltpu.VMEM)


def any_spec():
    return pl.BlockSpec(memory_space=pl.ANY)


def split_table(sources, local_freqs):
    total = sources * local_freqs
    freq = np.arange(total, dtype=np.float64).reshape(sources, 1, local_freqs)
    times = np.arange(STEPS, dtype=np.float64).reshape(STEPS, 1, 1, 1)
    phase = math.pi * times * freq[None] / total
    table = np.concatenate([np.cos(phase), -np.sin(phase)], axis=2) / math.sqrt(total)
    rest = table.reshape(STEPS, 2 * total).astype(np.float32)
    parts = []
    for _ in range(3):
        part = rest.astype(ml_dtypes.bfloat16)
        parts.append(part)
        rest = rest - part.astype(np.float32)
    return np.concatenate(parts, axis=0)


def prepare_kernel(table_ref, now_ref, before_ref, layer_ref, fk_ref, low_ref, high_ref, dealt_ref, mod_ref):
    for i in range(dealt_ref.shape[0]):
        for c in range(2):
            dealt_ref[i, pl.ds(2 * c, 2), :] = fk_ref[c, :, pl.ds(i * NPT, NPT)]

    def fill(x, _):
        level = layer_ref[x]
        modulus = jnp.full(level.shape, table_ref[0], jnp.float32)
        for k in range(1, table_ref.shape[0]):
            modulus = jnp.where(level == k, table_ref[k], modulus)
        mod_ref[x] = modulus
        return 0

    lax.fori_loop(0, CX, fill, 0, unroll=2)
    for k, ref in enumerate((now_ref, before_ref, mod_ref)):
        low_ref[pl.ds(k * CX, CX)] = ref[:, pl.ds(0, H), :]
        high_ref[pl.ds(k * CX, CX)] = ref[:, pl.ds(CY - H, H), :]


def middle_kernel(moved_ref, table_ref, owner_ref, cell_ref, now_hbm, before_hbm, mod_hbm, ylo_hbm, yhi_hbm,
                  out_ref, low_ref, high_ref, wide_ref, sems):
    copies = []
    for k, own in enumerate((now_hbm, before_hbm, mod_hbm)):
        for n, (slab, x) in enumerate(((low_ref, 0), (high_ref, CX - H))):
            rows = slab.at[pl.ds(k * H, H)]
            for m, (src, y, wide) in enumerate((
                (ylo_hbm.at[pl.ds(k * CX + x, H)], 0, H),
                (own.at[pl.ds(x, H)], H, CY),
                (yhi_hbm.at[pl.ds(k * CX + x, H)], H + CY, H),
            )):
                copies.append(pltpu.make_async_copy(src, rows.at[:, pl.ds(y, wide)], sems.at[k, n, m]))
    for c in copies:
        c.start()
    for i in range(moved_ref.shape[0]):
        wide_ref[pl.ds(4 * i, 4), :] = moved_ref[i].astype(jnp.float32)
    panel = wide_ref[...].astype(jnp.bfloat16)
    parts = jnp.dot(table_ref[...], panel, preferred_element_type=jnp.float32)
    force = parts[0:8] + parts[8:16] + parts[16:24]
    key = (owner_ref[...] * CELLS + cell_ref[...] + 1).astype(jnp.float32)
    keys = jnp.broadcast_to(key, (8, NPT))
    for a in range(out_ref.shape[0]):
        out_ref[a, 0:8, :] = force
        out_ref[a, 8:16, :] = keys
    for c in copies:
        c.wait()


def window_kernel(place_ref, now_hbm, before_hbm, mod_hbm, ylo_hbm, yhi_hbm, xlo_hbm, xhi_hbm,
                  fl_ref, fc_ref, fr_ref, next_hbm, prior_hbm,
                  a_ref, b_ref, m_ref, kx_ref, ky_ref, kz_ref, kc_ref, d_ref, code_ref, rank_ref, code_smem, rank_smem, list_smem,
                  sems, sem_code, sem_out):
    tiles = fc_ref.shape[0]
    copies = []
    for k, (own, ext) in enumerate(((now_hbm, a_ref), (before_hbm, b_ref), (mod_hbm, m_ref))):
        pieces = (
            (own, ext.at[pl.ds(1 + H, CX), pl.ds(2 * H, CY)]),
            (ylo_hbm.at[pl.ds(k * CX, CX)], ext.at[pl.ds(1 + H, CX), pl.ds(H, H)]),
            (yhi_hbm.at[pl.ds(k * CX, CX)], ext.at[pl.ds(1 + H, CX), pl.ds(2 * H + CY, H)]),
            (xlo_hbm.at[pl.ds(k * H, H)], ext.at[pl.ds(1, H), pl.ds(H, EY)]),
            (xhi_hbm.at[pl.ds(k * H, H)], ext.at[pl.ds(1 + H + CX, H), pl.ds(H, EY)]),
        )
        for n, (src, dst) in enumerate(pieces):
            copies.append(pltpu.make_async_copy(src, dst, sems.at[k, n]))
    for c in copies:
        c.start()

    my_y = place_ref[0]
    lane = lax.broadcasted_iota(jnp.int32, (tiles, NPT), 1)
    part = lax.broadcasted_iota(jnp.int32, (tiles, NPT), 0)
    for side, f_ref in enumerate((fl_ref, fc_ref, fr_ref)):
        key = f_ref[:, 8, :].astype(jnp.int32) - 1
        own = key >> 17
        cell = key & (CELLS - 1)
        gx = (cell >> 12) + (side - 1) * CX + H
        gy = (own - my_y) * CY + ((cell >> 7) & (CY - 1)) + H
        inside = (key >= 0) & (gx >= 1) & (gx < EX - 1) & (gy >= 1) & (gy < EY - 1)
        row = gx * EY + gy
        place = (side * tiles + part) * NPT + lane
        packed = (row << (Z_BITS + P_BITS)) | ((cell & (CZ - 1)) << P_BITS) | place
        code_ref[pl.ds(side * tiles, tiles), :] = jnp.where(inside, packed, -1)
    code = code_ref[...]
    found = jnp.where(code >= 0, 1.0, 0.0)
    ahead = jnp.where(
        lax.broadcasted_iota(jnp.int32, (NPT, NPT), 0) < lax.broadcasted_iota(jnp.int32, (NPT, NPT), 1), 1.0, 0.0)
    in_row = jnp.dot(found.astype(jnp.bfloat16), ahead.astype(jnp.bfloat16), preferred_element_type=jnp.float32)
    below = jnp.where(
        lax.broadcasted_iota(jnp.int32, (4 * tiles, 3 * tiles), 0) > lax.broadcasted_iota(jnp.int32, (4 * tiles, 3 * tiles), 1),
        1.0, 0.0)
    rows_before = jnp.dot(below.astype(jnp.bfloat16), found.astype(jnp.bfloat16), preferred_element_type=jnp.float32)
    before = jnp.sum(rows_before, axis=1, keepdims=True)
    rank_ref[pl.ds(0, 3 * tiles), :] = jnp.where(
        code >= 0, in_row + before[0:3 * tiles], 3.0 * tiles * NPT + GROUP).astype(jnp.int32)
    rank_ref[pl.ds(3 * tiles, tiles), :] = jnp.broadcast_to(before[3 * tiles:4 * tiles], (tiles, NPT)).astype(jnp.int32)
    code_copies = (
        pltpu.make_async_copy(code_ref, code_smem, sem_code.at[0]),
        pltpu.make_async_copy(rank_ref, rank_smem, sem_code.at[1]),
    )
    for c in code_copies:
        c.start()

    def clear(i, _):
        base = pl.multiple_of(i * 64, 64)
        for j in range(8):
            d_ref[pl.ds(base + 8 * j, 8), :] = jnp.zeros((8, CZ), jnp.float32)
        return 0

    lax.fori_loop(0, ROWS * STEPS // 64, clear, 0)
    for c in code_copies:
        c.wait()

    def pick_row(r, _):
        for c in range(NPT):
            list_smem[rank_smem[r, c]] = code_smem[r, c]
        return 0

    lax.fori_loop(0, 3 * tiles, pick_row, 0)
    count = rank_smem[3 * tiles, 0]
    for j in range(GROUP):
        list_smem[count + j] = 0

    zline = lax.broadcasted_iota(jnp.int32, (STEPS, CZ), 1)

    def add_points(i, _):
        adds = []
        for j in range(GROUP):
            code = list_smem[GROUP * i + j]
            place = code & ((1 << P_BITS) - 1)
            z = (code >> P_BITS) & (CZ - 1)
            row = code >> (Z_BITS + P_BITS)
            force = f_all[place >> 7, 0:8, :]
            column = jnp.take_along_axis(force, jnp.full((STEPS, CZ), place & (NPT - 1), jnp.int32), axis=1)
            adds.append((pl.ds(pl.multiple_of(row * STEPS, STEPS), STEPS), jnp.where(zline == z, column, 0.0)))
        for at, add in adds:
            d_ref[at, :] = d_ref[at, :] + add
        return 0

    f_all = kc_ref
    for side, f_ref in enumerate((fl_ref, fc_ref, fr_ref)):
        for a in range(tiles):
            kc_ref[side * tiles + a, 0:8, :] = f_ref[a, 0:8, :]
    lax.fori_loop(0, (count + GROUP - 1) // GROUP, add_points, 0)

    for c in copies:
        c.wait()

    zpos = lax.broadcasted_iota(jnp.int32, (8, CZ), 1)

    def face(c, n):
        return jnp.where(jnp.minimum(c, n) > 0.0, 0.075 * (c + n), 0.0)

    def coefficients(i, _):
        for k in range(8):
            x = 8 * i + k + 1
            for j in range(EY // 8):
                y = H + 8 * j
                c = m_ref[x, pl.ds(y, 8), :]
                xp = m_ref[x + 1, pl.ds(y, 8), :]
                xm = m_ref[x - 1, pl.ds(y, 8), :]
                yp = m_ref[x, pl.ds(y + 1, 8), :]
                ym = m_ref[x, pl.ds(y - 1, 8), :]
                zp = jnp.where(zpos == CZ - 1, 0.0, pltpu.roll(c, CZ - 1, 1))
                zm = jnp.where(zpos == 0, 0.0, pltpu.roll(c, 1, 1))
                kx_ref[x, pl.ds(y, 8), :] = face(c, xp)
                ky_ref[x, pl.ds(y, 8), :] = face(c, yp)
                kz_ref[x, pl.ds(y, 8), :] = face(c, zp)
                kc_ref[x, pl.ds(y, 8), :] = 2.0 - 0.075 * (6.0 * c + ((xp + xm) + (yp + ym) + (zp + zm)))
        return 0

    lax.fori_loop(0, EX // 8, coefficients, 0)

    next_copy, prior_copy = (
        pltpu.make_async_copy(ref.at[pl.ds(1 + H, CX), pl.ds(2 * H, CY)], hbm, sem_out.at[n])
        for n, (ref, hbm) in enumerate(((a_ref, next_hbm), (b_ref, prior_hbm)))
    )
    for step in range(STEPS):
        u_ref, w_ref = (a_ref, b_ref) if step % 2 == 0 else (b_ref, a_ref)

        planes = BODY[step]
        start = EX // 2 - 2 * planes
        rows = range(0, EY // 8) if step < STEPS - 1 else range(1, 1 + CY // 8)

        def advance(i, _, u_ref=u_ref, w_ref=w_ref, step=step, planes=planes, start=start, rows=rows):
            for k in range(planes):
                x = start + planes * i + k
                for j in rows:
                    y = H + 8 * j
                    u = u_ref[x + 1, pl.ds(y, 8), :]
                    kz = kz_ref[x + 1, pl.ds(y, 8), :]
                    in_z = kz * pltpu.roll(u, CZ - 1, 1) + pltpu.roll(kz * u, 1, 1)
                    in_x = (kx_ref[x + 1, pl.ds(y, 8), :] * u_ref[x + 2, pl.ds(y, 8), :]
                            + kx_ref[x, pl.ds(y, 8), :] * u_ref[x, pl.ds(y, 8), :])
                    in_y = (ky_ref[x + 1, pl.ds(y, 8), :] * u_ref[x + 1, pl.ds(y + 1, 8), :]
                            + ky_ref[x + 1, pl.ds(y - 1, 8), :] * u_ref[x + 1, pl.ds(y - 1, 8), :])
                    drive = d_ref[pl.ds((x * EY + 8 * j) * STEPS + step, 8, stride=STEPS), :]
                    own = kc_ref[x + 1, pl.ds(y, 8), :] * u - w_ref[x + 1, pl.ds(y, 8), :]
                    w_ref[x + 1, pl.ds(y, 8), :] = (own + drive) + ((in_x + in_y) + in_z)
            return 0

        lax.fori_loop(0, 4, advance, 0)

        if step == STEPS - 2:
            prior_copy.start()
    next_copy.start()
    next_copy.wait()
    prior_copy.wait()


def window(place, fields, forces):
    tiles = forces[0].shape[0]
    grid = jax.ShapeDtypeStruct((CX, CY, CZ), jnp.float32)
    buffer = pltpu.VMEM((EX + 2, PY, CZ), jnp.float32)
    return pl.pallas_call(
        window_kernel,
        out_shape=(grid, grid),
        in_specs=[pl.BlockSpec(memory_space=pltpu.SMEM)] + [any_spec()] * 7 + [vmem_spec()] * 3,
        out_specs=(any_spec(), any_spec()),
        scratch_shapes=[buffer] * 7 + [
            pltpu.VMEM((ROWS * STEPS, CZ), jnp.float32),
            pltpu.VMEM((3 * tiles, NPT), jnp.int32),
            pltpu.VMEM((4 * tiles, NPT), jnp.int32),
            pltpu.SMEM((3 * tiles, NPT), jnp.int32),
            pltpu.SMEM((4 * tiles, NPT), jnp.int32),
            pltpu.SMEM((3 * tiles * NPT + 2 * GROUP,), jnp.int32),
            pltpu.SemaphoreType.DMA((3, 5)),
            pltpu.SemaphoreType.DMA((2,)),
            pltpu.SemaphoreType.DMA((2,)),
        ],
        compiler_params=pltpu.CompilerParams(vmem_limit_bytes=LIMIT),
    )(place, *fields, *forces)


def neighbours(low, high, axis):
    count = lax.axis_size(axis)
    up = [(i, i + 1) for i in range(count - 1)]
    down = [(i + 1, i) for i in range(count - 1)]
    return lax.ppermute(high, axis, up), lax.ppermute(low, axis, down)


def shards(field_now, field_before, layer, modulus_table, fk_panel, owner, local_cell):
    sources, tiles = lax.axis_size("along"), lax.axis_size("across")
    local_freqs = fk_panel.shape[1]
    slab = jax.ShapeDtypeStruct((3 * CX, H, CZ), jnp.float32)
    low, high, dealt, modulus = pl.pallas_call(
        prepare_kernel,
        out_shape=(
            slab,
            slab,
            jax.ShapeDtypeStruct((sources, 2 * local_freqs, NPT), jnp.bfloat16),
            jax.ShapeDtypeStruct(field_now.shape, jnp.float32),
        ),
        in_specs=[pl.BlockSpec(memory_space=pltpu.SMEM)] + [vmem_spec()] * 4,
        out_specs=(vmem_spec(),) * 4,
        compiler_params=pltpu.CompilerParams(vmem_limit_bytes=LIMIT),
    )(modulus_table, field_now, field_before, layer, fk_panel.reshape(2, local_freqs, sources * NPT))
    arrays = (field_now, field_before, modulus)
    ylo, yhi = neighbours(low, high, "across")
    moved = lax.all_to_all(dealt, "along", 0, 0, tiled=True)
    ylo, yhi, moved = lax.optimization_barrier((ylo, yhi, moved))

    slab = jax.ShapeDtypeStruct((3 * H, EY, CZ), jnp.float32)
    payload, low, high = pl.pallas_call(
        middle_kernel,
        out_shape=(jax.ShapeDtypeStruct((tiles, 16, NPT), jnp.float32), slab, slab),
        in_specs=[vmem_spec()] * 4 + [any_spec()] * 5,
        out_specs=(vmem_spec(),) * 3,
        scratch_shapes=[
            pltpu.VMEM((2 * local_freqs * sources, NPT), jnp.float32),
            pltpu.SemaphoreType.DMA((3, 2, 3)),
        ],
        compiler_params=pltpu.CompilerParams(vmem_limit_bytes=LIMIT),
    )(moved, jnp.asarray(split_table(sources, local_freqs)), owner.reshape(1, NPT), local_cell, *arrays, ylo, yhi)
    xlo, xhi = neighbours(low, high, "along")
    center = lax.all_to_all(payload, "across", 0, 0, tiled=True)
    left, right = neighbours(center, center, "along")
    place = lax.axis_index("across").astype(jnp.int32).reshape(1)
    return window(place, (*arrays, ylo, yhi, xlo, xhi), (left, center, right))


def solution(mesh):
    placed = (
        P("along", "across", None),
        P("along", "across", None),
        P("along", "across", None),
        P(),
        P(None, "along", "across", None),
        P("across", "along", None),
        P("across", "along"),
    )
    return jax.shard_map(
        shards,
        mesh=mesh,
        in_specs=placed,
        out_specs=(P("along", "across", None), P("along", "across", None)),
        check_vma=False,
    )
```

```python
import math

import jax
import jax.numpy as jnp
import ml_dtypes
import numpy as np
from jax import lax
from jax.experimental import pallas as pl
from jax.experimental.pallas import tpu as pltpu
from jax.sharding import PartitionSpec as P

STEPS = 8
H = 8
CX, CY, CZ = 32, 32, 128
EX, EY = CX + 2 * H, CY + 2 * H
PY = EY + 2 * H
ROWS = EX * EY
CELLS = CX * CY * CZ
NPT = 128
ROW_BITS, Z_BITS, P_BITS = 12, 7, 12
BODY = (12, 11, 11, 10, 10, 9, 9, 8)
GROUP = 16
MIB = 1024 * 1024
PARTS = 4 * H


def vmem_spec():
    return pl.BlockSpec(memory_space=pltpu.VMEM)


def any_spec():
    return pl.BlockSpec(memory_space=pl.ANY)


def split_table(sources, local_freqs):
    total = sources * local_freqs
    freq = np.arange(total, dtype=np.float64).reshape(sources, 1, local_freqs)
    times = np.arange(STEPS, dtype=np.float64).reshape(STEPS, 1, 1, 1)
    phase = math.pi * times * freq[None] / total
    table = np.concatenate([np.cos(phase), -np.sin(phase)], axis=2) / math.sqrt(total)
    rest = table.reshape(STEPS, 2 * total).astype(np.float32)
    parts = []
    for _ in range(3):
        part = rest.astype(ml_dtypes.bfloat16)
        parts.append(part)
        rest = rest - part.astype(np.float32)
    return np.concatenate(parts, axis=0)


def prepare_kernel(table_ref, now_ref, before_ref, layer_ref, fk_ref, low_ref, high_ref, dealt_ref, mod_ref):
    for i in range(dealt_ref.shape[0]):
        for c in range(2):
            dealt_ref[i, pl.ds(2 * c, 2), :] = fk_ref[c, :, pl.ds(i * NPT, NPT)]

    def fill(x, _):
        level = layer_ref[x]
        modulus = jnp.full(level.shape, table_ref[0], jnp.float32)
        for k in range(1, table_ref.shape[0]):
            modulus = jnp.where(level == k, table_ref[k], modulus)
        mod_ref[x] = modulus
        return 0

    lax.fori_loop(0, CX, fill, 0, unroll=2)
    for k, ref in enumerate((now_ref, before_ref, mod_ref)):
        low_ref[pl.ds(k * CX, CX)] = ref[:, pl.ds(0, H), :]
        high_ref[pl.ds(k * CX, CX)] = ref[:, pl.ds(CY - H, H), :]


def transform_kernel(moved_ref, table_ref, owner_ref, cell_ref, out_ref, wide_ref):
    for i in range(moved_ref.shape[0]):
        wide_ref[pl.ds(4 * i, 4), :] = moved_ref[i].astype(jnp.float32)
    panel = wide_ref[...].astype(jnp.bfloat16)
    parts = jnp.dot(table_ref[...], panel, preferred_element_type=jnp.float32)
    out_ref[0:8, :] = parts[0:8] + parts[8:16] + parts[16:24]
    key = (owner_ref[...] * CELLS + cell_ref[...] + 1).astype(jnp.float32)
    out_ref[8:16, :] = jnp.broadcast_to(key, (8, NPT))


def spread_kernel(own_ref, left_ref, right_ref, now_hbm, before_hbm, mod_hbm, ylo_hbm, yhi_hbm,
                  out_ref, low_ref, high_ref, sems):
    copies = []
    for k, own in enumerate((now_hbm, before_hbm, mod_hbm)):
        for n, (slab, x) in enumerate(((low_ref, 0), (high_ref, CX - H))):
            rows = slab.at[pl.ds(k * H, H)]
            for m, (src, y, wide) in enumerate((
                (ylo_hbm.at[pl.ds(k * CX + x, H)], 0, H),
                (own.at[pl.ds(x, H)], H, CY),
                (yhi_hbm.at[pl.ds(k * CX + x, H)], H + CY, H),
            )):
                copies.append(pltpu.make_async_copy(src, rows.at[:, pl.ds(y, wide)], sems.at[k, n, m]))
    for c in copies:
        c.start()
    line = lax.broadcasted_iota(jnp.int32, (8, NPT), 0)
    keys = jnp.where(line == 0, own_ref[8:16, :], jnp.where(line == 1, left_ref[8:16, :], right_ref[8:16, :]))
    for a in range(out_ref.shape[0]):
        out_ref[a, 0:8, :] = own_ref[0:8, :]
        out_ref[a, 8:16, :] = left_ref[0:8, :]
        out_ref[a, 16:24, :] = right_ref[0:8, :]
        out_ref[a, 24:32, :] = keys
    for c in copies:
        c.wait()


def window_kernel(place_ref, now_hbm, before_hbm, mod_hbm, ylo_hbm, yhi_hbm, xlo_hbm, xhi_hbm,
                  got_ref, next_hbm, prior_hbm,
                  a_ref, b_ref, m_ref, kx_ref, ky_ref, kz_ref, kc_ref, d_ref, code_ref, code_smem, list_smem,
                  sems, sem_code, sem_out):
    tiles = got_ref.shape[0]
    copies = []
    for k, (own, ext) in enumerate(((now_hbm, a_ref), (before_hbm, b_ref), (mod_hbm, m_ref))):
        pieces = (
            (own, ext.at[pl.ds(1 + H, CX), pl.ds(2 * H, CY)]),
            (ylo_hbm.at[pl.ds(k * CX, CX)], ext.at[pl.ds(1 + H, CX), pl.ds(H, H)]),
            (yhi_hbm.at[pl.ds(k * CX, CX)], ext.at[pl.ds(1 + H, CX), pl.ds(2 * H + CY, H)]),
            (xlo_hbm.at[pl.ds(k * H, H)], ext.at[pl.ds(1, H), pl.ds(H, EY)]),
            (xhi_hbm.at[pl.ds(k * H, H)], ext.at[pl.ds(1 + H + CX, H), pl.ds(H, EY)]),
        )
        for n, (src, dst) in enumerate(pieces):
            copies.append(pltpu.make_async_copy(src, dst, sems.at[k, n]))
    for c in copies:
        c.start()

    my_y = place_ref[0]
    lane = lax.broadcasted_iota(jnp.int32, (tiles, NPT), 1)
    part = lax.broadcasted_iota(jnp.int32, (tiles, NPT), 0)
    codes = []
    for side in range(3):
        key = got_ref[:, 24 + side, :].astype(jnp.int32) - 1
        own = key >> 17
        cell = key & (CELLS - 1)
        gx = (cell >> 12) + (0, -CX, CX)[side] + H
        gy = (own - my_y) * CY + ((cell >> 7) & (CY - 1)) + H
        inside = (key >= 0) & (gx >= 1) & (gx < EX - 1) & (gy >= 1) & (gy < EY - 1)
        row = gx * EY + gy
        place = (part * 4 + side) * NPT + lane
        packed = (row << (Z_BITS + P_BITS)) | ((cell & (CZ - 1)) << P_BITS) | place
        codes.append(jnp.where(inside, packed, -1))

    rows = 3 * tiles
    code = jnp.concatenate(codes, axis=0)
    found = jnp.where(code >= 0, 1.0, 0.0)
    ahead = jnp.where(
        lax.broadcasted_iota(jnp.int32, (NPT, NPT), 0) < lax.broadcasted_iota(jnp.int32, (NPT, NPT), 1), 1.0, 0.0)
    rank = jnp.dot(found.astype(jnp.bfloat16), ahead.astype(jnp.bfloat16), preferred_element_type=jnp.float32)
    rank = jnp.where(code >= 0, rank, -1.0)
    held = jnp.maximum(code, 0)
    pieces = jnp.concatenate([(held >> (8 * k)) & 255 for k in range(4)], axis=0).astype(jnp.float32)
    slot = lax.broadcasted_iota(jnp.int32, (NPT, NPT), 0).astype(jnp.float32)
    which = lax.broadcasted_iota(jnp.int32, (rows, NPT), 0)
    which = jnp.concatenate([which] * 4, axis=0)
    front = jnp.zeros((4 * rows, NPT), jnp.float32)
    for r in range(rows):
        hot = jnp.where(jnp.broadcast_to(rank[r:r + 1, :], (NPT, NPT)) == slot, 1.0, 0.0).astype(jnp.bfloat16)
        mine = jnp.where(which == r, pieces, 0.0).astype(jnp.bfloat16)
        front = front + lax.dot_general(mine, hot, (((1,), (1,)), ((), ())), preferred_element_type=jnp.float32)
    front = front.astype(jnp.int32)
    ordered = front[0:rows]
    for k in range(1, 4):
        ordered = ordered | (front[k * rows:(k + 1) * rows] << (8 * k))
    code_ref[0:rows, :] = ordered
    code_ref[rows:2 * rows, :] = jnp.broadcast_to(jnp.sum(found, axis=1, keepdims=True), (rows, NPT)).astype(jnp.int32)
    code_copy = pltpu.make_async_copy(code_ref, code_smem, sem_code)
    code_copy.start()

    def clear(i, _):
        base = pl.multiple_of(i * 64, 64)
        for j in range(8):
            d_ref[pl.ds(base + 8 * j, 8), :] = jnp.zeros((8, CZ), jnp.float32)
        return 0

    lax.fori_loop(0, ROWS * STEPS // 64, clear, 0)
    code_copy.wait()

    def join_row(r, count):
        def move(i, _):
            for j in range(8):
                list_smem[count + 8 * i + j] = code_smem[r, 8 * i + j]
            return 0

        held_here = code_smem[rows + r, 0]
        lax.fori_loop(0, (held_here + 7) // 8, move, 0)
        return count + held_here

    count = lax.fori_loop(0, rows, join_row, 0)
    for j in range(GROUP):
        list_smem[count + j] = 0
    zline = lax.broadcasted_iota(jnp.int32, (STEPS, CZ), 1)

    def add_points(i, _):
        adds = []
        for j in range(GROUP):
            code = list_smem[GROUP * i + j]
            place = code & ((1 << P_BITS) - 1)
            z = (code >> P_BITS) & (CZ - 1)
            row = code >> (Z_BITS + P_BITS)
            side = (place >> 7) & 3
            force = got_ref[place >> 9, pl.ds(pl.multiple_of(side * STEPS, STEPS), STEPS), :]
            column = jnp.take_along_axis(force, jnp.full((STEPS, CZ), place & (NPT - 1), jnp.int32), axis=1)
            adds.append((pl.ds(pl.multiple_of(row * STEPS, STEPS), STEPS), jnp.where(zline == z, column, 0.0)))
        for at, add in adds:
            d_ref[at, :] = d_ref[at, :] + add
        return 0

    lax.fori_loop(0, (count + GROUP - 1) // GROUP, add_points, 0)

    for c in copies:
        c.wait()

    zpos = lax.broadcasted_iota(jnp.int32, (8, CZ), 1)

    def face(c, n):
        return jnp.where(jnp.minimum(c, n) > 0.0, 0.075 * (c + n), 0.0)

    def coefficients(i, _):
        for k in range(8):
            x = 8 * i + k + 1
            for j in range(EY // 8):
                y = H + 8 * j
                c = m_ref[x, pl.ds(y, 8), :]
                xp = m_ref[x + 1, pl.ds(y, 8), :]
                xm = m_ref[x - 1, pl.ds(y, 8), :]
                yp = m_ref[x, pl.ds(y + 1, 8), :]
                ym = m_ref[x, pl.ds(y - 1, 8), :]
                zp = jnp.where(zpos == CZ - 1, 0.0, pltpu.roll(c, CZ - 1, 1))
                zm = jnp.where(zpos == 0, 0.0, pltpu.roll(c, 1, 1))
                kx_ref[x, pl.ds(y, 8), :] = face(c, xp)
                ky_ref[x, pl.ds(y, 8), :] = face(c, yp)
                kz_ref[x, pl.ds(y, 8), :] = face(c, zp)
                kc_ref[x, pl.ds(y, 8), :] = 2.0 - 0.075 * (6.0 * c + ((xp + xm) + (yp + ym) + (zp + zm)))
        return 0

    lax.fori_loop(0, EX // 8, coefficients, 0)

    next_copy, prior_copy = (
        pltpu.make_async_copy(ref.at[pl.ds(1 + H, CX), pl.ds(2 * H, CY)], hbm, sem_out.at[n])
        for n, (ref, hbm) in enumerate(((a_ref, next_hbm), (b_ref, prior_hbm)))
    )
    for step in range(STEPS):
        u_ref, w_ref = (a_ref, b_ref) if step % 2 == 0 else (b_ref, a_ref)

        planes = BODY[step]
        start = EX // 2 - 2 * planes
        rows = range(0, EY // 8) if step < STEPS - 1 else range(1, 1 + CY // 8)

        def advance(i, _, u_ref=u_ref, w_ref=w_ref, step=step, planes=planes, start=start, rows=rows):
            for k in range(planes):
                x = start + planes * i + k
                for j in rows:
                    y = H + 8 * j
                    u = u_ref[x + 1, pl.ds(y, 8), :]
                    kz = kz_ref[x + 1, pl.ds(y, 8), :]
                    in_z = kz * pltpu.roll(u, CZ - 1, 1) + pltpu.roll(kz * u, 1, 1)
                    in_x = (kx_ref[x + 1, pl.ds(y, 8), :] * u_ref[x + 2, pl.ds(y, 8), :]
                            + kx_ref[x, pl.ds(y, 8), :] * u_ref[x, pl.ds(y, 8), :])
                    in_y = (ky_ref[x + 1, pl.ds(y, 8), :] * u_ref[x + 1, pl.ds(y + 1, 8), :]
                            + ky_ref[x + 1, pl.ds(y - 1, 8), :] * u_ref[x + 1, pl.ds(y - 1, 8), :])
                    drive = d_ref[pl.ds((x * EY + 8 * j) * STEPS + step, 8, stride=STEPS), :]
                    own = kc_ref[x + 1, pl.ds(y, 8), :] * u - w_ref[x + 1, pl.ds(y, 8), :]
                    w_ref[x + 1, pl.ds(y, 8), :] = (own + drive) + ((in_x + in_y) + in_z)
            return 0

        lax.fori_loop(0, 4, advance, 0)

        if step == STEPS - 2:
            prior_copy.start()
    next_copy.start()
    next_copy.wait()
    prior_copy.wait()


def window(place, fields, got):
    tiles = got.shape[0]
    grid = jax.ShapeDtypeStruct((CX, CY, CZ), jnp.float32)
    buffer = pltpu.VMEM((EX + 2, PY, CZ), jnp.float32)
    return pl.pallas_call(
        window_kernel,
        out_shape=(grid, grid),
        in_specs=[pl.BlockSpec(memory_space=pltpu.SMEM)] + [any_spec()] * 7 + [vmem_spec()],
        out_specs=(any_spec(), any_spec()),
        scratch_shapes=[buffer] * 7 + [
            pltpu.VMEM((ROWS * STEPS, CZ), jnp.float32),
            pltpu.VMEM((6 * tiles, NPT), jnp.int32),
            pltpu.SMEM((6 * tiles, NPT), jnp.int32),
            pltpu.SMEM((3 * tiles * NPT + 2 * GROUP,), jnp.int32),
            pltpu.SemaphoreType.DMA((3, 5)),
            pltpu.SemaphoreType.DMA,
            pltpu.SemaphoreType.DMA((2,)),
        ],
        compiler_params=pltpu.CompilerParams(vmem_limit_bytes=28 * MIB),
    )(place, *fields, got)


def neighbours(low, high, axis):
    count = lax.axis_size(axis)
    up = [(i, i + 1) for i in range(count - 1)]
    down = [(i + 1, i) for i in range(count - 1)]
    return lax.ppermute(high, axis, up), lax.ppermute(low, axis, down)


def shards(field_now, field_before, layer, modulus_table, fk_panel, owner, local_cell):
    sources, tiles = lax.axis_size("along"), lax.axis_size("across")
    local_freqs = fk_panel.shape[1]
    slab = jax.ShapeDtypeStruct((3 * CX, H, CZ), jnp.float32)
    low, high, dealt, modulus = pl.pallas_call(
        prepare_kernel,
        out_shape=(
            slab,
            slab,
            jax.ShapeDtypeStruct((sources, 2 * local_freqs, NPT), jnp.bfloat16),
            jax.ShapeDtypeStruct(field_now.shape, jnp.float32),
        ),
        in_specs=[pl.BlockSpec(memory_space=pltpu.SMEM)] + [vmem_spec()] * 4,
        out_specs=(vmem_spec(),) * 4,
        compiler_params=pltpu.CompilerParams(vmem_limit_bytes=58 * MIB),
    )(modulus_table, field_now, field_before, layer, fk_panel.reshape(2, local_freqs, sources * NPT))
    arrays = (field_now, field_before, modulus)
    ylo, yhi = neighbours(low, high, "across")
    moved = lax.all_to_all(dealt, "along", 0, 0, tiled=True)
    ylo, yhi, moved = lax.optimization_barrier((ylo, yhi, moved))

    samples = pl.pallas_call(
        transform_kernel,
        out_shape=jax.ShapeDtypeStruct((2 * STEPS, NPT), jnp.float32),
        in_specs=[vmem_spec()] * 4,
        out_specs=vmem_spec(),
        scratch_shapes=[pltpu.VMEM((2 * local_freqs * sources, NPT), jnp.float32)],
        compiler_params=pltpu.CompilerParams(vmem_limit_bytes=4 * MIB),
    )(moved, jnp.asarray(split_table(sources, local_freqs)), owner.reshape(1, NPT), local_cell)
    left, right = neighbours(samples, samples, "along")
    slab = jax.ShapeDtypeStruct((3 * H, EY, CZ), jnp.float32)
    spread, low, high = pl.pallas_call(
        spread_kernel,
        out_shape=(jax.ShapeDtypeStruct((tiles, PARTS, NPT), jnp.float32), slab, slab),
        in_specs=[vmem_spec()] * 3 + [any_spec()] * 5,
        out_specs=(vmem_spec(),) * 3,
        scratch_shapes=[pltpu.SemaphoreType.DMA((3, 2, 3))],
        compiler_params=pltpu.CompilerParams(vmem_limit_bytes=8 * MIB),
    )(samples, left, right, *arrays, ylo, yhi)
    xlo, xhi = neighbours(low, high, "along")
    got = lax.all_to_all(spread, "across", 0, 0, tiled=True)
    place = lax.axis_index("across").astype(jnp.int32).reshape(1)
    return window(place, (*arrays, ylo, yhi, xlo, xhi), got)


def solution(mesh):
    placed = (
        P("along", "across", None),
        P("along", "across", None),
        P("along", "across", None),
        P(),
        P(None, "along", "across", None),
        P("across", "along", None),
        P("across", "along"),
    )
    return jax.shard_map(
        shards,
        mesh=mesh,
        in_specs=placed,
        out_specs=(P("along", "across", None), P("along", "across", None)),
        check_vma=False,
    )
```

```python
import math

import jax
import jax.numpy as jnp
import ml_dtypes
import numpy as np
from jax import lax
from jax.experimental import pallas as pl
from jax.experimental.pallas import tpu as pltpu
from jax.sharding import PartitionSpec as P

STEPS = 8
H = 8
CX, CY, CZ = 32, 32, 128
EX, EY = CX + 2 * H, CY + 2 * H
PY = EY + 2 * H
ROWS = EX * EY
CELLS = CX * CY * CZ
NPT = 128
ROW_BITS, Z_BITS, P_BITS = 12, 7, 12
BODY = (12, 11, 11, 10, 10, 9, 9, 8)
GROUP = 32
MIB = 1024 * 1024
PARTS = 4 * H


def vmem_spec():
    return pl.BlockSpec(memory_space=pltpu.VMEM)


def any_spec():
    return pl.BlockSpec(memory_space=pl.ANY)


def split_table(sources, local_freqs):
    total = sources * local_freqs
    freq = np.arange(total, dtype=np.float64).reshape(sources, 1, local_freqs)
    times = np.arange(STEPS, dtype=np.float64).reshape(STEPS, 1, 1, 1)
    phase = math.pi * times * freq[None] / total
    table = np.concatenate([np.cos(phase), -np.sin(phase)], axis=2) / math.sqrt(total)
    rest = table.reshape(STEPS, 2 * total).astype(np.float32)
    parts = []
    for _ in range(3):
        part = rest.astype(ml_dtypes.bfloat16)
        parts.append(part)
        rest = rest - part.astype(np.float32)
    return np.concatenate(parts, axis=0)


def modulus_of(level, table_ref):
    modulus = jnp.full(level.shape, table_ref[0], jnp.float32)
    for k in range(1, table_ref.shape[0]):
        modulus = jnp.where(level == k, table_ref[k], modulus)
    return modulus


def prepare_kernel(table_ref, now_hbm, before_hbm, layer_hbm, fk_ref, low_ref, high_ref, dealt_ref, level_ref, sems):
    copies = []
    for n, (slab, y) in enumerate(((low_ref, 0), (high_ref, CY - H))):
        for k, (own, dst) in enumerate((
            (now_hbm, slab.at[pl.ds(0, CX)]),
            (before_hbm, slab.at[pl.ds(CX, CX)]),
            (layer_hbm, level_ref.at[n]),
        )):
            copies.append(pltpu.make_async_copy(own.at[:, pl.ds(y, H)], dst, sems.at[n, k]))
    for c in copies:
        c.start()
    for i in range(dealt_ref.shape[0]):
        for c in range(2):
            dealt_ref[i, pl.ds(2 * c, 2), :] = fk_ref[c, :, pl.ds(i * NPT, NPT)]
    for c in copies:
        c.wait()
    for n, slab in enumerate((low_ref, high_ref)):
        slab[pl.ds(2 * CX, CX)] = modulus_of(level_ref[n], table_ref)


def transform_kernel(moved_ref, table_ref, owner_ref, cell_ref, out_ref, wide_ref):
    for i in range(moved_ref.shape[0]):
        wide_ref[pl.ds(4 * i, 4), :] = moved_ref[i].astype(jnp.float32)
    panel = wide_ref[...].astype(jnp.bfloat16)
    parts = jnp.dot(table_ref[...], panel, preferred_element_type=jnp.float32)
    out_ref[0:8, :] = parts[0:8] + parts[8:16] + parts[16:24]
    key = (owner_ref[...] * CELLS + cell_ref[...] + 1).astype(jnp.float32)
    out_ref[8:16, :] = jnp.broadcast_to(key, (8, NPT))


def slab_kernel(table_ref, now_hbm, before_hbm, layer_hbm, ylo_hbm, yhi_hbm, low_ref, high_ref, level_ref, sems):
    copies = []
    for n, (slab, x) in enumerate(((low_ref, 0), (high_ref, CX - H))):
        for k, own in enumerate((now_hbm, before_hbm, layer_hbm)):
            rows = slab.at[pl.ds(k * H, H)]
            for m, (src, dst) in enumerate((
                (ylo_hbm.at[pl.ds(k * CX + x, H)], rows.at[:, pl.ds(0, H)]),
                (own.at[pl.ds(x, H)], level_ref.at[n] if k == 2 else rows.at[:, pl.ds(H, CY)]),
                (yhi_hbm.at[pl.ds(k * CX + x, H)], rows.at[:, pl.ds(H + CY, H)]),
            )):
                copies.append(pltpu.make_async_copy(src, dst, sems.at[k, n, m]))
    for c in copies:
        c.start()
    for c in copies:
        c.wait()
    for n, slab in enumerate((low_ref, high_ref)):
        slab[pl.ds(2 * H, H), pl.ds(H, CY), :] = modulus_of(level_ref[n], table_ref)


def spread_kernel(own_ref, left_ref, right_ref, out_hbm, out_ref, sem):
    line = lax.broadcasted_iota(jnp.int32, (8, NPT), 0)
    keys = jnp.where(line == 0, own_ref[8:16, :], jnp.where(line == 1, left_ref[8:16, :], right_ref[8:16, :]))
    for a in range(out_ref.shape[0]):
        out_ref[a, 0:8, :] = own_ref[0:8, :]
        out_ref[a, 8:16, :] = left_ref[0:8, :]
        out_ref[a, 16:24, :] = right_ref[0:8, :]
        out_ref[a, 24:32, :] = keys
    copy = pltpu.make_async_copy(out_ref, out_hbm, sem)
    copy.start()
    copy.wait()


def points_kernel(place_ref, got_ref, d_ref, code_ref, code_smem, list_smem, sem_code):
    tiles = got_ref.shape[0] // PARTS
    my_y = place_ref[0]
    lane = lax.broadcasted_iota(jnp.int32, (tiles, NPT), 1)
    part = lax.broadcasted_iota(jnp.int32, (tiles, NPT), 0)
    codes = []
    for side in range(3):
        key = got_ref[pl.ds(24 + side, tiles, stride=PARTS), :].astype(jnp.int32) - 1
        own = key >> 17
        cell = key & (CELLS - 1)
        gx = (cell >> 12) + (0, -CX, CX)[side] + H
        gy = (own - my_y) * CY + ((cell >> 7) & (CY - 1)) + H
        inside = (key >= 0) & (gx >= 1) & (gx < EX - 1) & (gy >= 1) & (gy < EY - 1)
        row = gx * EY + gy
        place = (part * 4 + side) * NPT + lane
        packed = (row << (Z_BITS + P_BITS)) | ((cell & (CZ - 1)) << P_BITS) | place
        codes.append(jnp.where(inside, packed, -1))

    rows = 3 * tiles
    code = jnp.concatenate(codes, axis=0)
    found = jnp.where(code >= 0, 1.0, 0.0)
    ahead = jnp.where(
        lax.broadcasted_iota(jnp.int32, (NPT, NPT), 0) < lax.broadcasted_iota(jnp.int32, (NPT, NPT), 1), 1.0, 0.0)
    rank = jnp.dot(found.astype(jnp.bfloat16), ahead.astype(jnp.bfloat16), preferred_element_type=jnp.float32)
    rank = jnp.where(code >= 0, rank, -1.0)
    held = jnp.maximum(code, 0)
    pieces = jnp.concatenate([(held >> (8 * k)) & 255 for k in range(4)], axis=0).astype(jnp.float32)
    slot = lax.broadcasted_iota(jnp.int32, (NPT, NPT), 0).astype(jnp.float32)
    which = lax.broadcasted_iota(jnp.int32, (rows, NPT), 0)
    which = jnp.concatenate([which] * 4, axis=0)
    front = jnp.zeros((4 * rows, NPT), jnp.float32)
    for r in range(rows):
        hot = jnp.where(jnp.broadcast_to(rank[r:r + 1, :], (NPT, NPT)) == slot, 1.0, 0.0).astype(jnp.bfloat16)
        mine = jnp.where(which == r, pieces, 0.0).astype(jnp.bfloat16)
        front = front + lax.dot_general(mine, hot, (((1,), (1,)), ((), ())), preferred_element_type=jnp.float32)
    front = front.astype(jnp.int32)
    ordered = front[0:rows]
    for k in range(1, 4):
        ordered = ordered | (front[k * rows:(k + 1) * rows] << (8 * k))
    code_ref[0:rows, :] = ordered
    code_ref[rows:2 * rows, :] = jnp.broadcast_to(jnp.sum(found, axis=1, keepdims=True), (rows, NPT)).astype(jnp.int32)
    code_copy = pltpu.make_async_copy(code_ref, code_smem, sem_code)
    code_copy.start()

    def clear(i, _):
        base = pl.multiple_of(i * 64, 64)
        for j in range(8):
            d_ref[pl.ds(base + 8 * j, 8), :] = jnp.zeros((8, CZ), jnp.float32)
        return 0

    lax.fori_loop(0, ROWS * STEPS // 64, clear, 0)
    code_copy.wait()

    def join_row(r, count):
        def move(i, _):
            for j in range(8):
                list_smem[count + 8 * i + j] = code_smem[r, 8 * i + j]
            return 0

        held_here = code_smem[rows + r, 0]
        lax.fori_loop(0, (held_here + 7) // 8, move, 0)
        return count + held_here

    count = lax.fori_loop(0, rows, join_row, 0)
    for j in range(GROUP):
        list_smem[count + j] = 0
    zline = lax.broadcasted_iota(jnp.int32, (STEPS, CZ), 1)

    def add_points(i, _):
        adds = []
        for j in range(GROUP):
            code = list_smem[GROUP * i + j]
            force = got_ref[pl.ds(pl.multiple_of((code >> 4) & (31 * STEPS), STEPS), STEPS), :]
            whole = jnp.full((STEPS, CZ), code, jnp.int32)
            column = jnp.take_along_axis(force, whole & (NPT - 1), axis=1, mode="promise_in_bounds")
            add = jnp.where(zline == ((whole >> P_BITS) & (CZ - 1)), column, 0.0)
            row = (code >> (Z_BITS + P_BITS - 3)) & -STEPS
            adds.append((pl.ds(pl.multiple_of(row, STEPS), STEPS), row, add))
        for first in range(0, GROUP, 4):
            part = adds[first:first + 4]
            sums = []
            for k, (at, row, add) in enumerate(part):
                total = d_ref[at, :] + add
                for _, other, more in part[:k]:
                    total = total + jnp.where(other == row, more, 0.0)
                sums.append(total)
            for (at, _, _), total in zip(part, sums):
                d_ref[at, :] = total
        return 0

    lax.fori_loop(0, (count + GROUP - 1) // GROUP, add_points, 0)


def window_kernel(table_ref, d_ref, now_hbm, before_hbm, layer_hbm, ylo_hbm, yhi_hbm, xlo_hbm, xhi_hbm,
                  next_hbm, prior_hbm, a_ref, b_ref, m_ref, kx_ref, ky_ref, kz_ref, kc_ref, level_ref, sems, sem_out):
    copies = []
    for k, (own, ext) in enumerate(((now_hbm, a_ref), (before_hbm, b_ref), (layer_hbm, m_ref))):
        pieces = (
            (own, level_ref if k == 2 else ext.at[pl.ds(1 + H, CX), pl.ds(2 * H, CY)]),
            (ylo_hbm.at[pl.ds(k * CX, CX)], ext.at[pl.ds(1 + H, CX), pl.ds(H, H)]),
            (yhi_hbm.at[pl.ds(k * CX, CX)], ext.at[pl.ds(1 + H, CX), pl.ds(2 * H + CY, H)]),
            (xlo_hbm.at[pl.ds(k * H, H)], ext.at[pl.ds(1, H), pl.ds(H, EY)]),
            (xhi_hbm.at[pl.ds(k * H, H)], ext.at[pl.ds(1 + H + CX, H), pl.ds(H, EY)]),
        )
        for n, (src, dst) in enumerate(pieces):
            copies.append(pltpu.make_async_copy(src, dst, sems.at[k, n]))
    for c in copies:
        c.start()
    for c in copies:
        c.wait()

    def fill(i, _):
        for k in range(4):
            x = 4 * i + k
            m_ref[1 + H + x, pl.ds(2 * H, CY), :] = modulus_of(level_ref[x], table_ref)
        return 0

    lax.fori_loop(0, CX // 4, fill, 0)
    zpos = lax.broadcasted_iota(jnp.int32, (8, CZ), 1)

    def face(c, n):
        return jnp.where(jnp.minimum(c, n) > 0.0, 0.075 * (c + n), 0.0)

    def coefficients(i, _):
        for k in range(8):
            x = 8 * i + k + 1
            for j in range(EY // 8):
                y = H + 8 * j
                c = m_ref[x, pl.ds(y, 8), :]
                xp = m_ref[x + 1, pl.ds(y, 8), :]
                xm = m_ref[x - 1, pl.ds(y, 8), :]
                yp = m_ref[x, pl.ds(y + 1, 8), :]
                ym = m_ref[x, pl.ds(y - 1, 8), :]
                zp = jnp.where(zpos == CZ - 1, 0.0, pltpu.roll(c, CZ - 1, 1))
                zm = jnp.where(zpos == 0, 0.0, pltpu.roll(c, 1, 1))
                kx_ref[x, pl.ds(y, 8), :] = face(c, xp)
                ky_ref[x, pl.ds(y, 8), :] = face(c, yp)
                kz_ref[x, pl.ds(y, 8), :] = face(c, zp)
                kc_ref[x, pl.ds(y, 8), :] = 2.0 - 0.075 * (6.0 * c + ((xp + xm) + (yp + ym) + (zp + zm)))
        return 0

    lax.fori_loop(0, EX // 8, coefficients, 0)

    next_copy, prior_copy = (
        pltpu.make_async_copy(ref.at[pl.ds(1 + H, CX), pl.ds(2 * H, CY)], hbm, sem_out.at[n])
        for n, (ref, hbm) in enumerate(((a_ref, next_hbm), (b_ref, prior_hbm)))
    )
    for step in range(STEPS):
        u_ref, w_ref = (a_ref, b_ref) if step % 2 == 0 else (b_ref, a_ref)

        planes = BODY[step]
        start = EX // 2 - 2 * planes
        rows = range(0, EY // 8) if step < STEPS - 1 else range(1, 1 + CY // 8)

        def advance(i, _, u_ref=u_ref, w_ref=w_ref, step=step, planes=planes, start=start, rows=rows):
            for k in range(planes):
                x = start + planes * i + k
                for j in rows:
                    y = H + 8 * j
                    u = u_ref[x + 1, pl.ds(y, 8), :]
                    kz = kz_ref[x + 1, pl.ds(y, 8), :]
                    in_z = kz * pltpu.roll(u, CZ - 1, 1) + pltpu.roll(kz * u, 1, 1)
                    in_x = (kx_ref[x + 1, pl.ds(y, 8), :] * u_ref[x + 2, pl.ds(y, 8), :]
                            + kx_ref[x, pl.ds(y, 8), :] * u_ref[x, pl.ds(y, 8), :])
                    in_y = (ky_ref[x + 1, pl.ds(y, 8), :] * u_ref[x + 1, pl.ds(y + 1, 8), :]
                            + ky_ref[x + 1, pl.ds(y - 1, 8), :] * u_ref[x + 1, pl.ds(y - 1, 8), :])
                    drive = d_ref[pl.ds((x * EY + 8 * j) * STEPS + step, 8, stride=STEPS), :]
                    own = kc_ref[x + 1, pl.ds(y, 8), :] * u - w_ref[x + 1, pl.ds(y, 8), :]
                    w_ref[x + 1, pl.ds(y, 8), :] = (own + drive) + ((in_x + in_y) + in_z)
            return 0

        lax.fori_loop(0, 4, advance, 0)

        if step == STEPS - 2:
            prior_copy.start()
    next_copy.start()
    next_copy.wait()
    prior_copy.wait()


def points(place, got):
    tiles = got.shape[0]
    return pl.pallas_call(
        points_kernel,
        out_shape=pltpu.VMEM((ROWS * STEPS, CZ), jnp.float32),
        in_specs=[pl.BlockSpec(memory_space=pltpu.SMEM), vmem_spec()],
        out_specs=vmem_spec(),
        scratch_shapes=[
            pltpu.VMEM((6 * tiles, NPT), jnp.int32),
            pltpu.SMEM((6 * tiles, NPT), jnp.int32),
            pltpu.SMEM((3 * tiles * NPT + 2 * GROUP,), jnp.int32),
            pltpu.SemaphoreType.DMA,
        ],
        cost_estimate=pl.CostEstimate(flops=10**9, transcendentals=0, bytes_accessed=64 * MIB),
        compiler_params=pltpu.CompilerParams(vmem_limit_bytes=4 * MIB),
    )(place, got.reshape(tiles * PARTS, NPT))


def window(table, drive, fields):
    grid = jax.ShapeDtypeStruct((CX, CY, CZ), jnp.float32)
    buffer = pltpu.VMEM((EX + 2, PY, CZ), jnp.float32)
    return pl.pallas_call(
        window_kernel,
        out_shape=(grid, grid),
        in_specs=[pl.BlockSpec(memory_space=pltpu.SMEM), vmem_spec()] + [any_spec()] * 7,
        out_specs=(any_spec(), any_spec()),
        scratch_shapes=[buffer] * 7 + [
            pltpu.VMEM((CX, CY, CZ), jnp.int32),
            pltpu.SemaphoreType.DMA((3, 5)),
            pltpu.SemaphoreType.DMA((2,)),
        ],
        compiler_params=pltpu.CompilerParams(vmem_limit_bytes=16 * MIB),
    )(table, pltpu.with_memory_space_constraint(drive, pltpu.VMEM), *fields)


def neighbours(low, high, axis):
    count = lax.axis_size(axis)
    up = [(i, i + 1) for i in range(count - 1)]
    down = [(i + 1, i) for i in range(count - 1)]
    return lax.ppermute(high, axis, up), lax.ppermute(low, axis, down)


def shards(field_now, field_before, layer, modulus_table, fk_panel, owner, local_cell):
    sources, tiles = lax.axis_size("along"), lax.axis_size("across")
    local_freqs = fk_panel.shape[1]
    arrays = (field_now, field_before, layer)
    smem = pl.BlockSpec(memory_space=pltpu.SMEM)
    slab = jax.ShapeDtypeStruct((3 * CX, H, CZ), jnp.float32)
    low, high, dealt = pl.pallas_call(
        prepare_kernel,
        out_shape=(slab, slab, jax.ShapeDtypeStruct((sources, 2 * local_freqs, NPT), jnp.bfloat16)),
        in_specs=[smem] + [any_spec()] * 3 + [vmem_spec()],
        out_specs=(vmem_spec(),) * 3,
        scratch_shapes=[pltpu.VMEM((2, CX, H, CZ), jnp.int32), pltpu.SemaphoreType.DMA((2, 3))],
        compiler_params=pltpu.CompilerParams(vmem_limit_bytes=58 * MIB),
    )(modulus_table, *arrays, fk_panel.reshape(2, local_freqs, sources * NPT))
    ylo, yhi = neighbours(low, high, "across")
    moved = lax.all_to_all(dealt, "along", 0, 0, tiled=True)
    ylo, yhi, moved = lax.optimization_barrier((ylo, yhi, moved))

    samples = pl.pallas_call(
        transform_kernel,
        out_shape=jax.ShapeDtypeStruct((2 * STEPS, NPT), jnp.float32),
        in_specs=[vmem_spec()] * 4,
        out_specs=vmem_spec(),
        scratch_shapes=[pltpu.VMEM((2 * local_freqs * sources, NPT), jnp.float32)],
        compiler_params=pltpu.CompilerParams(vmem_limit_bytes=58 * MIB),
    )(moved, jnp.asarray(split_table(sources, local_freqs)), owner.reshape(1, NPT), local_cell)
    left, right = neighbours(samples, samples, "along")
    spread = pl.pallas_call(
        spread_kernel,
        out_shape=pltpu.HBM((tiles, PARTS, NPT), jnp.float32),
        in_specs=[vmem_spec()] * 3,
        out_specs=pl.BlockSpec(memory_space=pltpu.HBM),
        scratch_shapes=[pltpu.VMEM((tiles, PARTS, NPT), jnp.float32), pltpu.SemaphoreType.DMA],
        compiler_params=pltpu.CompilerParams(vmem_limit_bytes=4 * MIB),
    )(samples, left, right)
    got = lax.all_to_all(spread, "across", 0, 0, tiled=True)
    slab = jax.ShapeDtypeStruct((3 * H, EY, CZ), jnp.float32)
    low, high = pl.pallas_call(
        slab_kernel,
        out_shape=(slab, slab),
        in_specs=[smem] + [any_spec()] * 5,
        out_specs=(vmem_spec(),) * 2,
        scratch_shapes=[pltpu.VMEM((2, H, CY, CZ), jnp.int32), pltpu.SemaphoreType.DMA((3, 2, 3))],
        compiler_params=pltpu.CompilerParams(vmem_limit_bytes=58 * MIB),
    )(modulus_table, *arrays, *lax.optimization_barrier((ylo, yhi, spread))[:2])
    xlo, xhi = neighbours(low, high, "along")
    place = lax.axis_index("across").astype(jnp.int32).reshape(1)
    drive = points(place, got)
    return window(modulus_table, drive, (*arrays, ylo, yhi, xlo, xhi))


def solution(mesh):
    placed = (
        P("along", "across", None),
        P("along", "across", None),
        P("along", "across", None),
        P(),
        P(None, "along", "across", None),
        P("across", "along", None),
        P("across", "along"),
    )
    return jax.shard_map(
        shards,
        mesh=mesh,
        in_specs=placed,
        out_specs=(P("along", "across", None), P("along", "across", None)),
        check_vma=False,
    )
```

```python
import math

import jax
import jax.numpy as jnp
import ml_dtypes
import numpy as np
from jax import lax
from jax.experimental import pallas as pl
from jax.experimental.pallas import tpu as pltpu
from jax.sharding import PartitionSpec as P

STEPS = 8
H = 8
CX, CY, CZ = 32, 32, 128
EX, EY = CX + 2 * H, CY + 2 * H
PY = EY + 2 * H
ROWS = EX * EY
CELLS = CX * CY * CZ
NPT = 128
ROW_BITS, Z_BITS, P_BITS = 12, 7, 12
BODY = (24, 22, 21, 20, 19, 18, 17, 16)
GROUP = 32
MIB = 1024 * 1024
PARTS = 4 * H


def vmem_spec():
    return pl.BlockSpec(memory_space=pltpu.VMEM)


def any_spec():
    return pl.BlockSpec(memory_space=pl.ANY)


def split_table(sources, local_freqs):
    total = sources * local_freqs
    freq = np.arange(total, dtype=np.float64).reshape(sources, 1, local_freqs)
    times = np.arange(STEPS, dtype=np.float64).reshape(STEPS, 1, 1, 1)
    phase = math.pi * times * freq[None] / total
    table = np.concatenate([np.cos(phase), -np.sin(phase)], axis=2) / math.sqrt(total)
    rest = table.reshape(STEPS, 2 * total).astype(np.float32)
    parts = []
    for _ in range(3):
        part = rest.astype(ml_dtypes.bfloat16)
        parts.append(part)
        rest = rest - part.astype(np.float32)
    return np.concatenate(parts, axis=0)


def modulus_of(level, table_ref):
    modulus = jnp.full(level.shape, table_ref[0], jnp.float32)
    for k in range(1, table_ref.shape[0]):
        modulus = jnp.where(level == k, table_ref[k], modulus)
    return modulus


def prepare_kernel(table_ref, now_hbm, before_hbm, layer_hbm, fk_ref, low_ref, high_ref, dealt_ref, level_ref, sems):
    copies = []
    for n, (slab, y) in enumerate(((low_ref, 0), (high_ref, CY - H))):
        for k, (own, dst) in enumerate((
            (now_hbm, slab.at[pl.ds(0, CX)]),
            (before_hbm, slab.at[pl.ds(CX, CX)]),
            (layer_hbm, level_ref.at[n]),
        )):
            copies.append(pltpu.make_async_copy(own.at[:, pl.ds(y, H)], dst, sems.at[n, k]))
    for c in copies:
        c.start()
    for i in range(dealt_ref.shape[0]):
        for c in range(2):
            dealt_ref[i, pl.ds(2 * c, 2), :] = fk_ref[c, :, pl.ds(i * NPT, NPT)]
    for c in copies:
        c.wait()
    for n, slab in enumerate((low_ref, high_ref)):
        slab[pl.ds(2 * CX, CX)] = modulus_of(level_ref[n], table_ref)


def transform_kernel(moved_ref, table_ref, owner_ref, cell_ref, out_ref, wide_ref):
    for i in range(moved_ref.shape[0]):
        wide_ref[pl.ds(4 * i, 4), :] = moved_ref[i].astype(jnp.float32)
    panel = wide_ref[...].astype(jnp.bfloat16)
    parts = jnp.dot(table_ref[...], panel, preferred_element_type=jnp.float32)
    out_ref[0:8, :] = parts[0:8] + parts[8:16] + parts[16:24]
    key = (owner_ref[...] * CELLS + cell_ref[...] + 1).astype(jnp.float32)
    out_ref[8:16, :] = jnp.broadcast_to(key, (8, NPT))


def slab_kernel(table_ref, now_hbm, before_hbm, layer_hbm, ylo_hbm, yhi_hbm, low_ref, high_ref, level_ref, sems):
    copies = []
    for n, (slab, x) in enumerate(((low_ref, 0), (high_ref, CX - H))):
        for k, own in enumerate((now_hbm, before_hbm, layer_hbm)):
            rows = slab.at[pl.ds(k * H, H)]
            for m, (src, dst) in enumerate((
                (ylo_hbm.at[pl.ds(k * CX + x, H)], rows.at[:, pl.ds(0, H)]),
                (own.at[pl.ds(x, H)], level_ref.at[n] if k == 2 else rows.at[:, pl.ds(H, CY)]),
                (yhi_hbm.at[pl.ds(k * CX + x, H)], rows.at[:, pl.ds(H + CY, H)]),
            )):
                copies.append(pltpu.make_async_copy(src, dst, sems.at[k, n, m]))
    for c in copies:
        c.start()
    for c in copies:
        c.wait()
    for n, slab in enumerate((low_ref, high_ref)):
        slab[pl.ds(2 * H, H), pl.ds(H, CY), :] = modulus_of(level_ref[n], table_ref)


def spread_kernel(own_ref, left_ref, right_ref, out_hbm, out_ref, sem):
    line = lax.broadcasted_iota(jnp.int32, (8, NPT), 0)
    keys = jnp.where(line == 0, own_ref[8:16, :], jnp.where(line == 1, left_ref[8:16, :], right_ref[8:16, :]))
    for a in range(out_ref.shape[0]):
        out_ref[a, 0:8, :] = own_ref[0:8, :]
        out_ref[a, 8:16, :] = left_ref[0:8, :]
        out_ref[a, 16:24, :] = right_ref[0:8, :]
        out_ref[a, 24:32, :] = keys
    copy = pltpu.make_async_copy(out_ref, out_hbm, sem)
    copy.start()
    copy.wait()


def points_kernel(place_ref, got_ref, d_ref, code_ref, code_smem, list_smem, sem_code):
    tiles = got_ref.shape[0] // PARTS
    my_y = place_ref[0]
    lane = lax.broadcasted_iota(jnp.int32, (tiles, NPT), 1)
    part = lax.broadcasted_iota(jnp.int32, (tiles, NPT), 0)
    codes = []
    for side in range(3):
        key = got_ref[pl.ds(24 + side, tiles, stride=PARTS), :].astype(jnp.int32) - 1
        own = key >> 17
        cell = key & (CELLS - 1)
        gx = (cell >> 12) + (0, -CX, CX)[side] + H
        gy = (own - my_y) * CY + ((cell >> 7) & (CY - 1)) + H
        inside = (key >= 0) & (gx >= 1) & (gx < EX - 1) & (gy >= 1) & (gy < EY - 1)
        row = gx * EY + gy
        place = (part * 4 + side) * NPT + lane
        packed = (row << (Z_BITS + P_BITS)) | ((cell & (CZ - 1)) << P_BITS) | place
        codes.append(jnp.where(inside, packed, -1))

    rows = 3 * tiles
    code = jnp.concatenate(codes, axis=0)
    found = jnp.where(code >= 0, 1.0, 0.0)
    ahead = jnp.where(
        lax.broadcasted_iota(jnp.int32, (NPT, NPT), 0) < lax.broadcasted_iota(jnp.int32, (NPT, NPT), 1), 1.0, 0.0)
    rank = jnp.dot(found.astype(jnp.bfloat16), ahead.astype(jnp.bfloat16), preferred_element_type=jnp.float32)
    rank = jnp.where(code >= 0, rank, -1.0)
    held = jnp.maximum(code, 0)
    pieces = jnp.concatenate([(held >> (8 * k)) & 255 for k in range(4)], axis=0).astype(jnp.float32)
    slot = lax.broadcasted_iota(jnp.int32, (NPT, NPT), 0).astype(jnp.float32)
    which = lax.broadcasted_iota(jnp.int32, (rows, NPT), 0)
    which = jnp.concatenate([which] * 4, axis=0)
    front = jnp.zeros((4 * rows, NPT), jnp.float32)
    for r in range(rows):
        hot = jnp.where(jnp.broadcast_to(rank[r:r + 1, :], (NPT, NPT)) == slot, 1.0, 0.0).astype(jnp.bfloat16)
        mine = jnp.where(which == r, pieces, 0.0).astype(jnp.bfloat16)
        front = front + lax.dot_general(mine, hot, (((1,), (1,)), ((), ())), preferred_element_type=jnp.float32)
    front = front.astype(jnp.int32)
    ordered = front[0:rows]
    for k in range(1, 4):
        ordered = ordered | (front[k * rows:(k + 1) * rows] << (8 * k))
    code_ref[0:rows, :] = ordered
    code_ref[rows:2 * rows, :] = jnp.broadcast_to(jnp.sum(found, axis=1, keepdims=True), (rows, NPT)).astype(jnp.int32)
    code_copy = pltpu.make_async_copy(code_ref, code_smem, sem_code)
    code_copy.start()

    def clear(i, _):
        base = pl.multiple_of(i * 64, 64)
        for j in range(8):
            d_ref[pl.ds(base + 8 * j, 8), :] = jnp.zeros((8, CZ), jnp.float32)
        return 0

    lax.fori_loop(0, ROWS * STEPS // 64, clear, 0)
    code_copy.wait()

    def join_row(r, count):
        def move(i, _):
            for j in range(8):
                list_smem[count + 8 * i + j] = code_smem[r, 8 * i + j]
            return 0

        held_here = code_smem[rows + r, 0]
        lax.fori_loop(0, (held_here + 7) // 8, move, 0)
        return count + held_here

    count = lax.fori_loop(0, rows, join_row, 0)
    for j in range(GROUP):
        list_smem[count + j] = 0
    zline = lax.broadcasted_iota(jnp.int32, (STEPS, CZ), 1)

    def add_points(i, _):
        adds = []
        for j in range(GROUP):
            code = list_smem[GROUP * i + j]
            force = got_ref[pl.ds(pl.multiple_of((code >> 4) & (31 * STEPS), STEPS), STEPS), :]
            whole = jnp.full((STEPS, CZ), code, jnp.int32)
            column = jnp.take_along_axis(force, whole & (NPT - 1), axis=1, mode="promise_in_bounds")
            add = jnp.where(zline == ((whole >> P_BITS) & (CZ - 1)), column, 0.0)
            row = (code >> (Z_BITS + P_BITS - 3)) & -STEPS
            adds.append((pl.ds(pl.multiple_of(row, STEPS), STEPS), row, add))
        for first in range(0, GROUP, 4):
            part = adds[first:first + 4]
            sums = []
            for k, (at, row, add) in enumerate(part):
                total = d_ref[at, :] + add
                for _, other, more in part[:k]:
                    total = total + jnp.where(other == row, more, 0.0)
                sums.append(total)
            for (at, _, _), total in zip(part, sums):
                d_ref[at, :] = total
        return 0

    lax.fori_loop(0, (count + GROUP - 1) // GROUP, add_points, 0)


def window_kernel(table_ref, d_ref, now_hbm, before_hbm, layer_hbm, ylo_hbm, yhi_hbm, xlo_hbm, xhi_hbm,
                  next_hbm, prior_hbm, a_ref, b_ref, m_ref, kx_ref, ky_ref, kz_ref, kc_ref, level_ref, sems, sem_out):
    copies = []
    for k, (own, ext) in enumerate(((now_hbm, a_ref), (before_hbm, b_ref), (layer_hbm, m_ref))):
        pieces = (
            (own, level_ref if k == 2 else ext.at[pl.ds(1 + H, CX), pl.ds(2 * H, CY)]),
            (ylo_hbm.at[pl.ds(k * CX, CX)], ext.at[pl.ds(1 + H, CX), pl.ds(H, H)]),
            (yhi_hbm.at[pl.ds(k * CX, CX)], ext.at[pl.ds(1 + H, CX), pl.ds(2 * H + CY, H)]),
            (xlo_hbm.at[pl.ds(k * H, H)], ext.at[pl.ds(1, H), pl.ds(H, EY)]),
            (xhi_hbm.at[pl.ds(k * H, H)], ext.at[pl.ds(1 + H + CX, H), pl.ds(H, EY)]),
        )
        for n, (src, dst) in enumerate(pieces):
            copies.append(pltpu.make_async_copy(src, dst, sems.at[k, n]))
    for c in copies:
        c.start()
    for c in copies:
        c.wait()

    def fill(i, _):
        for k in range(4):
            x = 4 * i + k
            m_ref[1 + H + x, pl.ds(2 * H, CY), :] = modulus_of(level_ref[x], table_ref)
        return 0

    lax.fori_loop(0, CX // 4, fill, 0)
    zpos = lax.broadcasted_iota(jnp.int32, (8, CZ), 1)

    def face(c, n):
        return jnp.where(jnp.minimum(c, n) > 0.0, 0.075 * (c + n), 0.0)

    def coefficients(i, _):
        for k in range(8):
            x = 8 * i + k + 1
            for j in range(EY // 8):
                y = H + 8 * j
                c = m_ref[x, pl.ds(y, 8), :]
                xp = m_ref[x + 1, pl.ds(y, 8), :]
                xm = m_ref[x - 1, pl.ds(y, 8), :]
                yp = m_ref[x, pl.ds(y + 1, 8), :]
                ym = m_ref[x, pl.ds(y - 1, 8), :]
                zp = jnp.where(zpos == CZ - 1, 0.0, pltpu.roll(c, CZ - 1, 1))
                zm = jnp.where(zpos == 0, 0.0, pltpu.roll(c, 1, 1))
                kx_ref[x, pl.ds(y, 8), :] = face(c, xp)
                ky_ref[x, pl.ds(y, 8), :] = face(c, yp)
                kz_ref[x, pl.ds(y, 8), :] = face(c, zp)
                kc_ref[x, pl.ds(y, 8), :] = 2.0 - 0.075 * (6.0 * c + ((xp + xm) + (yp + ym) + (zp + zm)))
        return 0

    lax.fori_loop(0, EX // 8, coefficients, 0)

    next_copy, prior_copy = (
        pltpu.make_async_copy(ref.at[pl.ds(1 + H, CX), pl.ds(2 * H, CY)], hbm, sem_out.at[n])
        for n, (ref, hbm) in enumerate(((a_ref, next_hbm), (b_ref, prior_hbm)))
    )
    for step in range(STEPS):
        u_ref, w_ref = (a_ref, b_ref) if step % 2 == 0 else (b_ref, a_ref)

        planes = BODY[step]
        start = EX // 2 - planes
        rows = range(0, EY // 8) if step < STEPS - 1 else range(1, 1 + CY // 8)

        def advance(i, _, u_ref=u_ref, w_ref=w_ref, step=step, planes=planes, start=start, rows=rows):
            for k in range(planes):
                x = start + planes * i + k
                for j in rows:
                    y = H + 8 * j
                    u = u_ref[x + 1, pl.ds(y, 8), :]
                    kz = kz_ref[x + 1, pl.ds(y, 8), :]
                    in_z = kz * pltpu.roll(u, CZ - 1, 1) + pltpu.roll(kz * u, 1, 1)
                    in_x = (kx_ref[x + 1, pl.ds(y, 8), :] * u_ref[x + 2, pl.ds(y, 8), :]
                            + kx_ref[x, pl.ds(y, 8), :] * u_ref[x, pl.ds(y, 8), :])
                    in_y = (ky_ref[x + 1, pl.ds(y, 8), :] * u_ref[x + 1, pl.ds(y + 1, 8), :]
                            + ky_ref[x + 1, pl.ds(y - 1, 8), :] * u_ref[x + 1, pl.ds(y - 1, 8), :])
                    drive = d_ref[pl.ds((x * EY + 8 * j) * STEPS + step, 8, stride=STEPS), :]
                    own = kc_ref[x + 1, pl.ds(y, 8), :] * u - w_ref[x + 1, pl.ds(y, 8), :]
                    w_ref[x + 1, pl.ds(y, 8), :] = (own + drive) + ((in_x + in_y) + in_z)
            return 0

        lax.fori_loop(0, 2, advance, 0)

        if step == STEPS - 2:
            prior_copy.start()
    next_copy.start()
    next_copy.wait()
    prior_copy.wait()


def points(place, got):
    tiles = got.shape[0]
    return pl.pallas_call(
        points_kernel,
        out_shape=pltpu.VMEM((ROWS * STEPS, CZ), jnp.float32),
        in_specs=[pl.BlockSpec(memory_space=pltpu.SMEM), vmem_spec()],
        out_specs=vmem_spec(),
        scratch_shapes=[
            pltpu.VMEM((6 * tiles, NPT), jnp.int32),
            pltpu.SMEM((6 * tiles, NPT), jnp.int32),
            pltpu.SMEM((3 * tiles * NPT + 2 * GROUP,), jnp.int32),
            pltpu.SemaphoreType.DMA,
        ],
        cost_estimate=pl.CostEstimate(flops=10**12, transcendentals=0, bytes_accessed=1024 * MIB),
        compiler_params=pltpu.CompilerParams(vmem_limit_bytes=4 * MIB),
    )(place, got.reshape(tiles * PARTS, NPT))


def window(table, drive, fields):
    grid = jax.ShapeDtypeStruct((CX, CY, CZ), jnp.float32)
    buffer = pltpu.VMEM((EX + 2, PY, CZ), jnp.float32)
    return pl.pallas_call(
        window_kernel,
        out_shape=(grid, grid),
        in_specs=[pl.BlockSpec(memory_space=pltpu.SMEM), vmem_spec()] + [any_spec()] * 7,
        out_specs=(any_spec(), any_spec()),
        scratch_shapes=[buffer] * 7 + [
            pltpu.VMEM((CX, CY, CZ), jnp.int32),
            pltpu.SemaphoreType.DMA((3, 5)),
            pltpu.SemaphoreType.DMA((2,)),
        ],
        compiler_params=pltpu.CompilerParams(vmem_limit_bytes=16 * MIB),
    )(table, pltpu.with_memory_space_constraint(drive, pltpu.VMEM), *fields)


def neighbours(low, high, axis):
    count = lax.axis_size(axis)
    up = [(i, i + 1) for i in range(count - 1)]
    down = [(i + 1, i) for i in range(count - 1)]
    return lax.ppermute(high, axis, up), lax.ppermute(low, axis, down)


def shards(field_now, field_before, layer, modulus_table, fk_panel, owner, local_cell):
    sources, tiles = lax.axis_size("along"), lax.axis_size("across")
    local_freqs = fk_panel.shape[1]
    arrays = (field_now, field_before, layer)
    smem = pl.BlockSpec(memory_space=pltpu.SMEM)
    slab = pltpu.VMEM((3 * CX, H, CZ), jnp.float32)
    low, high, dealt = pl.pallas_call(
        prepare_kernel,
        out_shape=(slab, slab, pltpu.VMEM((sources, 2 * local_freqs, NPT), jnp.bfloat16)),
        in_specs=[smem] + [any_spec()] * 3 + [vmem_spec()],
        out_specs=(vmem_spec(),) * 3,
        scratch_shapes=[pltpu.VMEM((2, CX, H, CZ), jnp.int32), pltpu.SemaphoreType.DMA((2, 3))],
        compiler_params=pltpu.CompilerParams(vmem_limit_bytes=58 * MIB),
    )(modulus_table, *arrays, fk_panel.reshape(2, local_freqs, sources * NPT))
    ylo, yhi = neighbours(low, high, "across")
    moved = lax.all_to_all(dealt, "along", 0, 0, tiled=True)
    ylo, yhi, moved = lax.optimization_barrier((ylo, yhi, moved))

    samples = pl.pallas_call(
        transform_kernel,
        out_shape=pltpu.VMEM((2 * STEPS, NPT), jnp.float32),
        in_specs=[vmem_spec()] * 4,
        out_specs=vmem_spec(),
        scratch_shapes=[pltpu.VMEM((2 * local_freqs * sources, NPT), jnp.float32)],
        compiler_params=pltpu.CompilerParams(vmem_limit_bytes=58 * MIB),
    )(moved, jnp.asarray(split_table(sources, local_freqs)), owner.reshape(1, NPT), local_cell)
    left, right = neighbours(samples, samples, "along")
    spread = pl.pallas_call(
        spread_kernel,
        out_shape=pltpu.HBM((tiles, PARTS, NPT), jnp.float32),
        in_specs=[vmem_spec()] * 3,
        out_specs=pl.BlockSpec(memory_space=pltpu.HBM),
        scratch_shapes=[pltpu.VMEM((tiles, PARTS, NPT), jnp.float32), pltpu.SemaphoreType.DMA],
        compiler_params=pltpu.CompilerParams(vmem_limit_bytes=4 * MIB),
    )(samples, left, right)
    got = lax.all_to_all(spread, "across", 0, 0, tiled=True)
    slab = jax.ShapeDtypeStruct((3 * H, EY, CZ), jnp.float32)
    low, high = pl.pallas_call(
        slab_kernel,
        out_shape=(slab, slab),
        in_specs=[smem] + [any_spec()] * 5,
        out_specs=(vmem_spec(),) * 2,
        scratch_shapes=[pltpu.VMEM((2, H, CY, CZ), jnp.int32), pltpu.SemaphoreType.DMA((3, 2, 3))],
        compiler_params=pltpu.CompilerParams(vmem_limit_bytes=58 * MIB),
    )(modulus_table, *arrays, *lax.optimization_barrier((ylo, yhi, samples))[:2])
    xlo, xhi = neighbours(low, high, "along")
    place = lax.axis_index("across").astype(jnp.int32).reshape(1)
    drive = points(place, got)
    return window(modulus_table, drive, (*arrays, ylo, yhi, xlo, xhi))


def solution(mesh):
    placed = (
        P("along", "across", None),
        P("along", "across", None),
        P("along", "across", None),
        P(),
        P(None, "along", "across", None),
        P("across", "along", None),
        P("across", "along"),
    )
    return jax.shard_map(
        shards,
        mesh=mesh,
        in_specs=placed,
        out_specs=(P("along", "across", None), P("along", "across", None)),
        check_vma=False,
    )
```

```python
import math

import jax
import jax.numpy as jnp
import ml_dtypes
import numpy as np
from jax import lax
from jax.experimental import pallas as pl
from jax.experimental.pallas import tpu as pltpu
from jax.sharding import PartitionSpec as P

STEPS = 8
H = 8
CX, CY, CZ = 32, 32, 128
EX, EY = CX + 2 * H, CY + 2 * H
PY = EY + 2 * H
ROWS = EX * EY
CELLS = CX * CY * CZ
NPT = 128
ROW_BITS, Z_BITS, P_BITS = 12, 7, 12
BODY = (24, 22, 21, 20, 19, 18, 17, 16)
GROUP = 32
MIB = 1024 * 1024
PARTS = 4 * H


def vmem_spec():
    return pl.BlockSpec(memory_space=pltpu.VMEM)


def any_spec():
    return pl.BlockSpec(memory_space=pl.ANY)


def split_table(sources, local_freqs):
    total = sources * local_freqs
    freq = np.arange(total, dtype=np.float64).reshape(sources, 1, local_freqs)
    times = np.arange(STEPS, dtype=np.float64).reshape(STEPS, 1, 1, 1)
    phase = math.pi * times * freq[None] / total
    table = np.concatenate([np.cos(phase), -np.sin(phase)], axis=2) / math.sqrt(total)
    rest = table.reshape(STEPS, 2 * total).astype(np.float32)
    parts = []
    for _ in range(3):
        part = rest.astype(ml_dtypes.bfloat16)
        parts.append(part)
        rest = rest - part.astype(np.float32)
    return np.concatenate(parts, axis=0)


def modulus_of(level, table_ref):
    modulus = jnp.full(level.shape, table_ref[0], jnp.float32)
    for k in range(1, table_ref.shape[0]):
        modulus = jnp.where(level == k, table_ref[k], modulus)
    return modulus


def prepare_kernel(table_ref, now_hbm, before_hbm, layer_hbm, fk_ref, low_ref, high_ref, dealt_ref, level_ref, sems):
    copies = []
    for n, (slab, y) in enumerate(((low_ref, 0), (high_ref, CY - H))):
        for k, (own, dst) in enumerate((
            (now_hbm, slab.at[pl.ds(0, CX)]),
            (before_hbm, slab.at[pl.ds(CX, CX)]),
            (layer_hbm, level_ref.at[n]),
        )):
            copies.append(pltpu.make_async_copy(own.at[:, pl.ds(y, H)], dst, sems.at[n, k]))
    for c in copies:
        c.start()
    for i in range(dealt_ref.shape[0]):
        for c in range(2):
            dealt_ref[i, pl.ds(2 * c, 2), :] = fk_ref[c, :, pl.ds(i * NPT, NPT)]
    for c in copies:
        c.wait()
    for n, slab in enumerate((low_ref, high_ref)):
        slab[pl.ds(2 * CX, CX)] = modulus_of(level_ref[n], table_ref)


def transform_kernel(moved_ref, table_ref, owner_ref, cell_ref, out_ref, wide_ref):
    for i in range(moved_ref.shape[0]):
        wide_ref[pl.ds(4 * i, 4), :] = moved_ref[i].astype(jnp.float32)
    panel = wide_ref[...].astype(jnp.bfloat16)
    parts = jnp.dot(table_ref[...], panel, preferred_element_type=jnp.float32)
    out_ref[0:8, :] = parts[0:8] + parts[8:16] + parts[16:24]
    key = (owner_ref[...] * CELLS + cell_ref[...] + 1).astype(jnp.float32)
    out_ref[8:16, :] = jnp.broadcast_to(key, (8, NPT))


def slab_kernel(table_ref, now_hbm, before_hbm, layer_hbm, ylo_hbm, yhi_hbm, low_ref, high_ref, level_ref, sems):
    copies = []
    for n, (slab, x) in enumerate(((low_ref, 0), (high_ref, CX - H))):
        for k, own in enumerate((now_hbm, before_hbm, layer_hbm)):
            rows = slab.at[pl.ds(k * H, H)]
            for m, (src, dst) in enumerate((
                (ylo_hbm.at[pl.ds(k * CX + x, H)], rows.at[:, pl.ds(0, H)]),
                (own.at[pl.ds(x, H)], level_ref.at[n] if k == 2 else rows.at[:, pl.ds(H, CY)]),
                (yhi_hbm.at[pl.ds(k * CX + x, H)], rows.at[:, pl.ds(H + CY, H)]),
            )):
                copies.append(pltpu.make_async_copy(src, dst, sems.at[k, n, m]))
    for c in copies:
        c.start()
    for c in copies:
        c.wait()
    for n, slab in enumerate((low_ref, high_ref)):
        slab[pl.ds(2 * H, H), pl.ds(H, CY), :] = modulus_of(level_ref[n], table_ref)


def spread_kernel(own_ref, left_ref, right_ref, out_hbm, out_ref, sem):
    line = lax.broadcasted_iota(jnp.int32, (8, NPT), 0)
    keys = jnp.where(line == 0, own_ref[8:16, :], jnp.where(line == 1, left_ref[8:16, :], right_ref[8:16, :]))
    for a in range(out_ref.shape[0]):
        out_ref[a, 0:8, :] = own_ref[0:8, :]
        out_ref[a, 8:16, :] = left_ref[0:8, :]
        out_ref[a, 16:24, :] = right_ref[0:8, :]
        out_ref[a, 24:32, :] = keys
    copy = pltpu.make_async_copy(out_ref, out_hbm, sem)
    copy.start()
    copy.wait()


def points_kernel(place_ref, got_ref, d_ref, code_ref, code_smem, list_smem, sem_code):
    tiles = got_ref.shape[0] // PARTS
    my_y = place_ref[0]
    lane = lax.broadcasted_iota(jnp.int32, (tiles, NPT), 1)
    part = lax.broadcasted_iota(jnp.int32, (tiles, NPT), 0)
    codes = []
    for side in range(3):
        key = got_ref[pl.ds(24 + side, tiles, stride=PARTS), :].astype(jnp.int32) - 1
        own = key >> 17
        cell = key & (CELLS - 1)
        gx = (cell >> 12) + (0, -CX, CX)[side] + H
        gy = (own - my_y) * CY + ((cell >> 7) & (CY - 1)) + H
        inside = (key >= 0) & (gx >= 1) & (gx < EX - 1) & (gy >= 1) & (gy < EY - 1)
        row = gx * EY + gy
        place = (part * 4 + side) * NPT + lane
        packed = (row << (Z_BITS + P_BITS)) | ((cell & (CZ - 1)) << P_BITS) | place
        codes.append(jnp.where(inside, packed, -1))

    rows = 3 * tiles
    code = jnp.concatenate(codes, axis=0)
    found = jnp.where(code >= 0, 1.0, 0.0)
    ahead = jnp.where(
        lax.broadcasted_iota(jnp.int32, (NPT, NPT), 0) < lax.broadcasted_iota(jnp.int32, (NPT, NPT), 1), 1.0, 0.0)
    rank = jnp.dot(found.astype(jnp.bfloat16), ahead.astype(jnp.bfloat16), preferred_element_type=jnp.float32)
    rank = jnp.where(code >= 0, rank, -1.0)
    held = jnp.maximum(code, 0)
    pieces = jnp.concatenate([(held >> (8 * k)) & 255 for k in range(4)], axis=0).astype(jnp.float32)
    slot = lax.broadcasted_iota(jnp.int32, (NPT, NPT), 0).astype(jnp.float32)
    which = lax.broadcasted_iota(jnp.int32, (rows, NPT), 0)
    which = jnp.concatenate([which] * 4, axis=0)
    front = jnp.zeros((4 * rows, NPT), jnp.float32)
    for r in range(rows):
        hot = jnp.where(jnp.broadcast_to(rank[r:r + 1, :], (NPT, NPT)) == slot, 1.0, 0.0).astype(jnp.bfloat16)
        mine = jnp.where(which == r, pieces, 0.0).astype(jnp.bfloat16)
        front = front + lax.dot_general(mine, hot, (((1,), (1,)), ((), ())), preferred_element_type=jnp.float32)
    front = front.astype(jnp.int32)
    ordered = front[0:rows]
    for k in range(1, 4):
        ordered = ordered | (front[k * rows:(k + 1) * rows] << (8 * k))
    code_ref[0:rows, :] = ordered
    code_ref[rows:2 * rows, :] = jnp.broadcast_to(jnp.sum(found, axis=1, keepdims=True), (rows, NPT)).astype(jnp.int32)
    code_copy = pltpu.make_async_copy(code_ref, code_smem, sem_code)
    code_copy.start()

    def clear(i, _):
        base = pl.multiple_of(i * 64, 64)
        for j in range(8):
            d_ref[pl.ds(base + 8 * j, 8), :] = jnp.zeros((8, CZ), jnp.float32)
        return 0

    lax.fori_loop(0, ROWS * STEPS // 64, clear, 0)
    code_copy.wait()

    def join_row(r, count):
        def move(i, _):
            for j in range(8):
                list_smem[count + 8 * i + j] = code_smem[r, 8 * i + j]
            return 0

        held_here = code_smem[rows + r, 0]
        lax.fori_loop(0, (held_here + 7) // 8, move, 0)
        return count + held_here

    count = lax.fori_loop(0, rows, join_row, 0)
    for j in range(GROUP):
        list_smem[count + j] = 0
    zline = lax.broadcasted_iota(jnp.int32, (STEPS, CZ), 1)

    def add_points(i, _):
        adds = []
        for j in range(GROUP):
            code = list_smem[GROUP * i + j]
            force = got_ref[pl.ds(pl.multiple_of((code >> 4) & (31 * STEPS), STEPS), STEPS), :]
            whole = jnp.full((STEPS, CZ), code, jnp.int32)
            column = jnp.take_along_axis(force, whole & (NPT - 1), axis=1, mode="promise_in_bounds")
            add = jnp.where(zline == ((whole >> P_BITS) & (CZ - 1)), column, 0.0)
            row = (code >> (Z_BITS + P_BITS - 3)) & -STEPS
            adds.append((pl.ds(pl.multiple_of(row, STEPS), STEPS), row, add))
        for first in range(0, GROUP, 4):
            part = adds[first:first + 4]
            sums = []
            for k, (at, row, add) in enumerate(part):
                total = d_ref[at, :] + add
                for _, other, more in part[:k]:
                    total = total + jnp.where(other == row, more, 0.0)
                sums.append(total)
            for (at, _, _), total in zip(part, sums):
                d_ref[at, :] = total
        return 0

    lax.fori_loop(0, (count + GROUP - 1) // GROUP, add_points, 0)


def window_kernel(table_ref, d_ref, now_hbm, before_hbm, layer_hbm, ylo_hbm, yhi_hbm, xlo_hbm, xhi_hbm,
                  next_hbm, prior_hbm, a_ref, b_ref, m_ref, kx_ref, ky_ref, kz_ref, kc_ref, level_ref, sems, sem_out):
    copies = []
    for k, (own, ext) in enumerate(((now_hbm, a_ref), (before_hbm, b_ref), (layer_hbm, m_ref))):
        pieces = (
            (own, level_ref if k == 2 else ext.at[pl.ds(1 + H, CX), pl.ds(2 * H, CY)]),
            (ylo_hbm.at[pl.ds(k * CX, CX)], ext.at[pl.ds(1 + H, CX), pl.ds(H, H)]),
            (yhi_hbm.at[pl.ds(k * CX, CX)], ext.at[pl.ds(1 + H, CX), pl.ds(2 * H + CY, H)]),
            (xlo_hbm.at[pl.ds(k * H, H)], ext.at[pl.ds(1, H), pl.ds(H, EY)]),
            (xhi_hbm.at[pl.ds(k * H, H)], ext.at[pl.ds(1 + H + CX, H), pl.ds(H, EY)]),
        )
        for n, (src, dst) in enumerate(pieces):
            copies.append(pltpu.make_async_copy(src, dst, sems.at[k, n]))
    for c in copies:
        c.start()
    for c in copies:
        c.wait()

    def fill(i, _):
        for k in range(4):
            x = 4 * i + k
            m_ref[1 + H + x, pl.ds(2 * H, CY), :] = modulus_of(level_ref[x], table_ref)
        return 0

    lax.fori_loop(0, CX // 4, fill, 0)
    zpos = lax.broadcasted_iota(jnp.int32, (8, CZ), 1)

    def face(c, n):
        return jnp.where(jnp.minimum(c, n) > 0.0, 0.075 * (c + n), 0.0)

    def coefficients(i, _):
        for k in range(8):
            x = 8 * i + k + 1
            for j in range(EY // 8):
                y = H + 8 * j
                c = m_ref[x, pl.ds(y, 8), :]
                xp = m_ref[x + 1, pl.ds(y, 8), :]
                xm = m_ref[x - 1, pl.ds(y, 8), :]
                yp = m_ref[x, pl.ds(y + 1, 8), :]
                ym = m_ref[x, pl.ds(y - 1, 8), :]
                zp = jnp.where(zpos == CZ - 1, 0.0, pltpu.roll(c, CZ - 1, 1))
                zm = jnp.where(zpos == 0, 0.0, pltpu.roll(c, 1, 1))
                kx_ref[x, pl.ds(y, 8), :] = face(c, xp)
                ky_ref[x, pl.ds(y, 8), :] = face(c, yp)
                kz_ref[x, pl.ds(y, 8), :] = face(c, zp)
                kc_ref[x, pl.ds(y, 8), :] = 2.0 - 0.075 * (6.0 * c + ((xp + xm) + (yp + ym) + (zp + zm)))
        return 0

    lax.fori_loop(0, EX // 8, coefficients, 0)

    next_copy, prior_copy = (
        pltpu.make_async_copy(ref.at[pl.ds(1 + H, CX), pl.ds(2 * H, CY)], hbm, sem_out.at[n])
        for n, (ref, hbm) in enumerate(((a_ref, next_hbm), (b_ref, prior_hbm)))
    )
    for step in range(STEPS):
        u_ref, w_ref = (a_ref, b_ref) if step % 2 == 0 else (b_ref, a_ref)

        planes = BODY[step]
        start = EX // 2 - planes
        rows = range(0, EY // 8) if step < STEPS - 1 else range(1, 1 + CY // 8)

        def advance(i, _, u_ref=u_ref, w_ref=w_ref, step=step, planes=planes, start=start, rows=rows):
            for k in range(planes):
                x = start + planes * i + k
                for j in rows:
                    y = H + 8 * j
                    u = u_ref[x + 1, pl.ds(y, 8), :]
                    kz = kz_ref[x + 1, pl.ds(y, 8), :]
                    in_z = kz * pltpu.roll(u, CZ - 1, 1) + pltpu.roll(kz * u, 1, 1)
                    in_x = (kx_ref[x + 1, pl.ds(y, 8), :] * u_ref[x + 2, pl.ds(y, 8), :]
                            + kx_ref[x, pl.ds(y, 8), :] * u_ref[x, pl.ds(y, 8), :])
                    in_y = (ky_ref[x + 1, pl.ds(y, 8), :] * u_ref[x + 1, pl.ds(y + 1, 8), :]
                            + ky_ref[x + 1, pl.ds(y - 1, 8), :] * u_ref[x + 1, pl.ds(y - 1, 8), :])
                    drive = d_ref[pl.ds((x * EY + 8 * j) * STEPS + step, 8, stride=STEPS), :]
                    own = kc_ref[x + 1, pl.ds(y, 8), :] * u - w_ref[x + 1, pl.ds(y, 8), :]
                    w_ref[x + 1, pl.ds(y, 8), :] = (own + drive) + ((in_x + in_y) + in_z)
            return 0

        lax.fori_loop(0, 2, advance, 0)

        if step == STEPS - 2:
            prior_copy.start()
    next_copy.start()
    next_copy.wait()
    prior_copy.wait()


def points(place, got):
    tiles = got.shape[0]
    return pl.pallas_call(
        points_kernel,
        out_shape=pltpu.VMEM((ROWS * STEPS, CZ), jnp.float32),
        in_specs=[pl.BlockSpec(memory_space=pltpu.SMEM), vmem_spec()],
        out_specs=vmem_spec(),
        scratch_shapes=[
            pltpu.VMEM((6 * tiles, NPT), jnp.int32),
            pltpu.SMEM((6 * tiles, NPT), jnp.int32),
            pltpu.SMEM((3 * tiles * NPT + 2 * GROUP,), jnp.int32),
            pltpu.SemaphoreType.DMA,
        ],
        cost_estimate=pl.CostEstimate(flops=10**6, transcendentals=0, bytes_accessed=10 * MIB),
        compiler_params=pltpu.CompilerParams(vmem_limit_bytes=4 * MIB),
    )(place, got.reshape(tiles * PARTS, NPT))


def window(table, drive, fields):
    grid = jax.ShapeDtypeStruct((CX, CY, CZ), jnp.float32)
    buffer = pltpu.VMEM((EX + 2, PY, CZ), jnp.float32)
    return pl.pallas_call(
        window_kernel,
        out_shape=(grid, grid),
        in_specs=[pl.BlockSpec(memory_space=pltpu.SMEM), vmem_spec()] + [any_spec()] * 7,
        out_specs=(any_spec(), any_spec()),
        scratch_shapes=[buffer] * 7 + [
            pltpu.VMEM((CX, CY, CZ), jnp.int32),
            pltpu.SemaphoreType.DMA((3, 5)),
            pltpu.SemaphoreType.DMA((2,)),
        ],
        compiler_params=pltpu.CompilerParams(vmem_limit_bytes=16 * MIB),
    )(table, pltpu.with_memory_space_constraint(drive, pltpu.VMEM), *fields)


def neighbours(low, high, axis):
    count = lax.axis_size(axis)
    up = [(i, i + 1) for i in range(count - 1)]
    down = [(i + 1, i) for i in range(count - 1)]
    return lax.ppermute(high, axis, up), lax.ppermute(low, axis, down)


def shards(field_now, field_before, layer, modulus_table, fk_panel, owner, local_cell):
    sources, tiles = lax.axis_size("along"), lax.axis_size("across")
    local_freqs = fk_panel.shape[1]
    arrays = (field_now, field_before, layer)
    smem = pl.BlockSpec(memory_space=pltpu.SMEM)
    slab = pltpu.VMEM((3 * CX, H, CZ), jnp.float32)
    low, high, dealt = pl.pallas_call(
        prepare_kernel,
        out_shape=(slab, slab, pltpu.VMEM((sources, 2 * local_freqs, NPT), jnp.bfloat16)),
        in_specs=[smem] + [any_spec()] * 3 + [vmem_spec()],
        out_specs=(vmem_spec(),) * 3,
        scratch_shapes=[pltpu.VMEM((2, CX, H, CZ), jnp.int32), pltpu.SemaphoreType.DMA((2, 3))],
        compiler_params=pltpu.CompilerParams(vmem_limit_bytes=58 * MIB),
    )(modulus_table, *arrays, fk_panel.reshape(2, local_freqs, sources * NPT))
    ylo, yhi = neighbours(low, high, "across")
    moved = lax.all_to_all(dealt, "along", 0, 0, tiled=True)
    ylo, yhi, moved = lax.optimization_barrier((ylo, yhi, moved))

    samples = pl.pallas_call(
        transform_kernel,
        out_shape=pltpu.VMEM((2 * STEPS, NPT), jnp.float32),
        in_specs=[vmem_spec()] * 4,
        out_specs=vmem_spec(),
        scratch_shapes=[pltpu.VMEM((2 * local_freqs * sources, NPT), jnp.float32)],
        compiler_params=pltpu.CompilerParams(vmem_limit_bytes=58 * MIB),
    )(moved, jnp.asarray(split_table(sources, local_freqs)), owner.reshape(1, NPT), local_cell)
    left, right = neighbours(samples, samples, "along")
    slab = pltpu.VMEM((3 * H, EY, CZ), jnp.float32)
    low, high = pl.pallas_call(
        slab_kernel,
        out_shape=(slab, slab),
        in_specs=[smem] + [any_spec()] * 5,
        out_specs=(vmem_spec(),) * 2,
        scratch_shapes=[pltpu.VMEM((2, H, CY, CZ), jnp.int32), pltpu.SemaphoreType.DMA((3, 2, 3))],
        compiler_params=pltpu.CompilerParams(vmem_limit_bytes=58 * MIB),
    )(modulus_table, *arrays, *lax.optimization_barrier((ylo, yhi, samples))[:2])
    low, high, left, right = lax.optimization_barrier((low, high, left, right))
    xlo, xhi = neighbours(low, high, "along")
    spread = pl.pallas_call(
        spread_kernel,
        out_shape=pltpu.HBM((tiles, PARTS, NPT), jnp.float32),
        in_specs=[vmem_spec()] * 3,
        out_specs=pl.BlockSpec(memory_space=pltpu.HBM),
        scratch_shapes=[pltpu.VMEM((tiles, PARTS, NPT), jnp.float32), pltpu.SemaphoreType.DMA],
        compiler_params=pltpu.CompilerParams(vmem_limit_bytes=4 * MIB),
    )(samples, left, right)
    got = lax.all_to_all(spread, "across", 0, 0, tiled=True)
    place = lax.axis_index("across").astype(jnp.int32).reshape(1)
    drive = points(place, got)
    return window(modulus_table, drive, (*arrays, ylo, yhi, xlo, xhi))


def solution(mesh):
    placed = (
        P("along", "across", None),
        P("along", "across", None),
        P("along", "across", None),
        P(),
        P(None, "along", "across", None),
        P("across", "along", None),
        P("across", "along"),
    )
    return jax.shard_map(
        shards,
        mesh=mesh,
        in_specs=placed,
        out_specs=(P("along", "across", None), P("along", "across", None)),
        check_vma=False,
    )
```

```python
import math

import jax
import jax.numpy as jnp
import ml_dtypes
import numpy as np
from jax import lax
from jax.experimental import pallas as pl
from jax.experimental.pallas import tpu as pltpu
from jax.sharding import PartitionSpec as P

STEPS = 8
H = 8
CX, CY, CZ = 32, 32, 128
EX, EY = CX + 2 * H, CY + 2 * H
PY = EY + 2 * H
ROWS = EX * EY
CELLS = CX * CY * CZ
NPT = 128
ROW_BITS, Z_BITS, P_BITS = 12, 7, 12
PLANES = (48, 44, 42, 40, 38, 36, 34, 32)
GROUP = 32
MIB = 1024 * 1024
PARTS = 4 * H


def vmem_spec():
    return pl.BlockSpec(memory_space=pltpu.VMEM)


def any_spec():
    return pl.BlockSpec(memory_space=pl.ANY)


def split_table(sources, local_freqs):
    total = sources * local_freqs
    freq = np.arange(total, dtype=np.float64).reshape(sources, 1, local_freqs)
    times = np.arange(STEPS, dtype=np.float64).reshape(STEPS, 1, 1, 1)
    phase = math.pi * times * freq[None] / total
    table = np.concatenate([np.cos(phase), -np.sin(phase)], axis=2) / math.sqrt(total)
    rest = table.reshape(STEPS, 2 * total).astype(np.float32)
    parts = []
    for _ in range(3):
        part = rest.astype(ml_dtypes.bfloat16)
        parts.append(part)
        rest = rest - part.astype(np.float32)
    return np.concatenate(parts, axis=0)


def modulus_of(level, table_ref):
    modulus = jnp.full(level.shape, table_ref[0], jnp.float32)
    for k in range(1, table_ref.shape[0]):
        modulus = jnp.where(level == k, table_ref[k], modulus)
    return modulus


def prepare_kernel(table_ref, now_hbm, before_hbm, layer_hbm, fk_ref, low_ref, high_ref, dealt_ref, level_ref, sems):
    copies = []
    for n, (slab, y) in enumerate(((low_ref, 0), (high_ref, CY - H))):
        for k, (own, dst) in enumerate((
            (now_hbm, slab.at[pl.ds(0, CX)]),
            (before_hbm, slab.at[pl.ds(CX, CX)]),
            (layer_hbm, level_ref.at[n]),
        )):
            copies.append(pltpu.make_async_copy(own.at[:, pl.ds(y, H)], dst, sems.at[n, k]))
    for c in copies:
        c.start()
    for i in range(dealt_ref.shape[0]):
        for c in range(2):
            dealt_ref[i, pl.ds(2 * c, 2), :] = fk_ref[c, :, pl.ds(i * NPT, NPT)]
    for c in copies:
        c.wait()
    for n, slab in enumerate((low_ref, high_ref)):
        slab[pl.ds(2 * CX, CX)] = modulus_of(level_ref[n], table_ref)


def transform_kernel(moved_ref, table_ref, owner_ref, cell_ref, out_ref, wide_ref):
    for i in range(moved_ref.shape[0]):
        wide_ref[pl.ds(4 * i, 4), :] = moved_ref[i].astype(jnp.float32)
    panel = wide_ref[...].astype(jnp.bfloat16)
    parts = jnp.dot(table_ref[...], panel, preferred_element_type=jnp.float32)
    out_ref[0:8, :] = parts[0:8] + parts[8:16] + parts[16:24]
    key = (owner_ref[...] * CELLS + cell_ref[...] + 1).astype(jnp.float32)
    out_ref[8:16, :] = jnp.broadcast_to(key, (8, NPT))


def slab_kernel(table_ref, now_hbm, before_hbm, layer_hbm, ylo_hbm, yhi_hbm, low_ref, high_ref, level_ref, sems):
    copies = []
    for n, (slab, x) in enumerate(((low_ref, 0), (high_ref, CX - H))):
        for k, own in enumerate((now_hbm, before_hbm, layer_hbm)):
            rows = slab.at[pl.ds(k * H, H)]
            for m, (src, dst) in enumerate((
                (ylo_hbm.at[pl.ds(k * CX + x, H)], rows.at[:, pl.ds(0, H)]),
                (own.at[pl.ds(x, H)], level_ref.at[n] if k == 2 else rows.at[:, pl.ds(H, CY)]),
                (yhi_hbm.at[pl.ds(k * CX + x, H)], rows.at[:, pl.ds(H + CY, H)]),
            )):
                copies.append(pltpu.make_async_copy(src, dst, sems.at[k, n, m]))
    for c in copies:
        c.start()
    for c in copies:
        c.wait()
    for n, slab in enumerate((low_ref, high_ref)):
        slab[pl.ds(2 * H, H), pl.ds(H, CY), :] = modulus_of(level_ref[n], table_ref)


def spread_kernel(own_ref, left_ref, right_ref, out_hbm, out_ref, sem):
    line = lax.broadcasted_iota(jnp.int32, (8, NPT), 0)
    keys = jnp.where(line == 0, own_ref[8:16, :], jnp.where(line == 1, left_ref[8:16, :], right_ref[8:16, :]))
    for a in range(out_ref.shape[0]):
        out_ref[a, 0:8, :] = own_ref[0:8, :]
        out_ref[a, 8:16, :] = left_ref[0:8, :]
        out_ref[a, 16:24, :] = right_ref[0:8, :]
        out_ref[a, 24:32, :] = keys
    copy = pltpu.make_async_copy(out_ref, out_hbm, sem)
    copy.start()
    copy.wait()


def points_kernel(place_ref, got_ref, d_ref, code_ref, code_smem, list_smem, sem_code):
    tiles = got_ref.shape[0] // PARTS
    my_y = place_ref[0]
    lane = lax.broadcasted_iota(jnp.int32, (tiles, NPT), 1)
    part = lax.broadcasted_iota(jnp.int32, (tiles, NPT), 0)
    codes = []
    for side in range(3):
        key = got_ref[pl.ds(24 + side, tiles, stride=PARTS), :].astype(jnp.int32) - 1
        own = key >> 17
        cell = key & (CELLS - 1)
        gx = (cell >> 12) + (0, -CX, CX)[side] + H
        gy = (own - my_y) * CY + ((cell >> 7) & (CY - 1)) + H
        inside = (key >= 0) & (gx >= 1) & (gx < EX - 1) & (gy >= 1) & (gy < EY - 1)
        row = gx * EY + gy
        place = (part * 4 + side) * NPT + lane
        packed = (row << (Z_BITS + P_BITS)) | ((cell & (CZ - 1)) << P_BITS) | place
        codes.append(jnp.where(inside, packed, -1))

    rows = 3 * tiles
    code = jnp.concatenate(codes, axis=0)
    found = jnp.where(code >= 0, 1.0, 0.0)
    ahead = jnp.where(
        lax.broadcasted_iota(jnp.int32, (NPT, NPT), 0) < lax.broadcasted_iota(jnp.int32, (NPT, NPT), 1), 1.0, 0.0)
    rank = jnp.dot(found.astype(jnp.bfloat16), ahead.astype(jnp.bfloat16), preferred_element_type=jnp.float32)
    rank = jnp.where(code >= 0, rank, -1.0)
    held = jnp.maximum(code, 0)
    pieces = jnp.concatenate([(held >> (8 * k)) & 255 for k in range(4)], axis=0).astype(jnp.float32)
    slot = lax.broadcasted_iota(jnp.int32, (NPT, NPT), 0).astype(jnp.float32)
    which = lax.broadcasted_iota(jnp.int32, (rows, NPT), 0)
    which = jnp.concatenate([which] * 4, axis=0)
    front = jnp.zeros((4 * rows, NPT), jnp.float32)
    for r in range(rows):
        hot = jnp.where(jnp.broadcast_to(rank[r:r + 1, :], (NPT, NPT)) == slot, 1.0, 0.0).astype(jnp.bfloat16)
        mine = jnp.where(which == r, pieces, 0.0).astype(jnp.bfloat16)
        front = front + lax.dot_general(mine, hot, (((1,), (1,)), ((), ())), preferred_element_type=jnp.float32)
    front = front.astype(jnp.int32)
    ordered = front[0:rows]
    for k in range(1, 4):
        ordered = ordered | (front[k * rows:(k + 1) * rows] << (8 * k))
    code_ref[0:rows, :] = ordered
    code_ref[rows:2 * rows, :] = jnp.broadcast_to(jnp.sum(found, axis=1, keepdims=True), (rows, NPT)).astype(jnp.int32)
    code_copy = pltpu.make_async_copy(code_ref, code_smem, sem_code)
    code_copy.start()

    def clear(i, _):
        base = pl.multiple_of(i * 64, 64)
        for j in range(8):
            d_ref[pl.ds(base + 8 * j, 8), :] = jnp.zeros((8, CZ), jnp.float32)
        return 0

    lax.fori_loop(0, ROWS * STEPS // 64, clear, 0)
    code_copy.wait()

    def join_row(r, count):
        def move(i, _):
            for j in range(8):
                list_smem[count + 8 * i + j] = code_smem[r, 8 * i + j]
            return 0

        held_here = code_smem[rows + r, 0]
        lax.fori_loop(0, (held_here + 7) // 8, move, 0)
        return count + held_here

    count = lax.fori_loop(0, rows, join_row, 0)
    for j in range(GROUP):
        list_smem[count + j] = 0
    zline = lax.broadcasted_iota(jnp.int32, (STEPS, CZ), 1)

    def add_points(i, _):
        adds = []
        for j in range(GROUP):
            code = list_smem[GROUP * i + j]
            force = got_ref[pl.ds(pl.multiple_of((code >> 4) & (31 * STEPS), STEPS), STEPS), :]
            whole = jnp.full((STEPS, CZ), code, jnp.int32)
            column = jnp.take_along_axis(force, whole & (NPT - 1), axis=1, mode="promise_in_bounds")
            add = jnp.where(zline == ((whole >> P_BITS) & (CZ - 1)), column, 0.0)
            row = (code >> (Z_BITS + P_BITS - 3)) & -STEPS
            adds.append((pl.ds(pl.multiple_of(row, STEPS), STEPS), row, add))
        for first in range(0, GROUP, 4):
            part = adds[first:first + 4]
            sums = []
            for k, (at, row, add) in enumerate(part):
                total = d_ref[at, :] + add
                for _, other, more in part[:k]:
                    total = total + jnp.where(other == row, more, 0.0)
                sums.append(total)
            for (at, _, _), total in zip(part, sums):
                d_ref[at, :] = total
        return 0

    lax.fori_loop(0, (count + GROUP - 1) // GROUP, add_points, 0)


def window_kernel(table_ref, d_ref, now_hbm, before_hbm, layer_hbm, ylo_hbm, yhi_hbm, xlo_hbm, xhi_hbm,
                  next_hbm, prior_hbm, a_ref, b_ref, m_ref, kx_ref, ky_ref, kz_ref, kc_ref, level_ref, sems, sem_out):
    copies = []
    for k, (own, ext) in enumerate(((now_hbm, a_ref), (before_hbm, b_ref), (layer_hbm, m_ref))):
        pieces = (
            (own, level_ref if k == 2 else ext.at[pl.ds(1 + H, CX), pl.ds(2 * H, CY)]),
            (ylo_hbm.at[pl.ds(k * CX, CX)], ext.at[pl.ds(1 + H, CX), pl.ds(H, H)]),
            (yhi_hbm.at[pl.ds(k * CX, CX)], ext.at[pl.ds(1 + H, CX), pl.ds(2 * H + CY, H)]),
            (xlo_hbm.at[pl.ds(k * H, H)], ext.at[pl.ds(1, H), pl.ds(H, EY)]),
            (xhi_hbm.at[pl.ds(k * H, H)], ext.at[pl.ds(1 + H + CX, H), pl.ds(H, EY)]),
        )
        for n, (src, dst) in enumerate(pieces):
            copies.append(pltpu.make_async_copy(src, dst, sems.at[k, n]))
    fields, layers = copies[:10], copies[10:]
    for c in layers + fields:
        c.start()
    for c in layers:
        c.wait()

    def fill(i, _):
        for k in range(4):
            x = 4 * i + k
            m_ref[1 + H + x, pl.ds(2 * H, CY), :] = modulus_of(level_ref[x], table_ref)
        return 0

    lax.fori_loop(0, CX // 4, fill, 0)
    zpos = lax.broadcasted_iota(jnp.int32, (8, CZ), 1)

    def face(c, n):
        return jnp.where(jnp.minimum(c, n) > 0.0, 0.075 * (c + n), 0.0)

    def coefficients(i, _):
        for k in range(8):
            x = 8 * i + k + 1
            for j in range(EY // 8):
                y = H + 8 * j
                c = m_ref[x, pl.ds(y, 8), :]
                xp = m_ref[x + 1, pl.ds(y, 8), :]
                xm = m_ref[x - 1, pl.ds(y, 8), :]
                yp = m_ref[x, pl.ds(y + 1, 8), :]
                ym = m_ref[x, pl.ds(y - 1, 8), :]
                zp = jnp.where(zpos == CZ - 1, 0.0, pltpu.roll(c, CZ - 1, 1))
                zm = jnp.where(zpos == 0, 0.0, pltpu.roll(c, 1, 1))
                kx_ref[x, pl.ds(y, 8), :] = face(c, xp)
                ky_ref[x, pl.ds(y, 8), :] = face(c, yp)
                kz_ref[x, pl.ds(y, 8), :] = face(c, zp)
                kc_ref[x, pl.ds(y, 8), :] = 2.0 - 0.075 * (6.0 * c + ((xp + xm) + (yp + ym) + (zp + zm)))
        return 0

    lax.fori_loop(0, EX // 8, coefficients, 0)
    for c in fields:
        c.wait()

    next_copy, prior_copy = (
        pltpu.make_async_copy(ref.at[pl.ds(1 + H, CX), pl.ds(2 * H, CY)], hbm, sem_out.at[n])
        for n, (ref, hbm) in enumerate(((a_ref, next_hbm), (b_ref, prior_hbm)))
    )
    for step in range(STEPS):
        u_ref, w_ref = (a_ref, b_ref) if step % 2 == 0 else (b_ref, a_ref)

        planes = PLANES[step]
        start = EX // 2 - planes // 2
        rows = range(0, EY // 8) if step < STEPS - 1 else range(1, 1 + CY // 8)

        for x in range(start, start + planes):
            for j in rows:
                y = H + 8 * j
                u = u_ref[x + 1, pl.ds(y, 8), :]
                kz = kz_ref[x + 1, pl.ds(y, 8), :]
                in_z = kz * pltpu.roll(u, CZ - 1, 1) + pltpu.roll(kz * u, 1, 1)
                in_x = (kx_ref[x + 1, pl.ds(y, 8), :] * u_ref[x + 2, pl.ds(y, 8), :]
                        + kx_ref[x, pl.ds(y, 8), :] * u_ref[x, pl.ds(y, 8), :])
                in_y = (ky_ref[x + 1, pl.ds(y, 8), :] * u_ref[x + 1, pl.ds(y + 1, 8), :]
                        + ky_ref[x + 1, pl.ds(y - 1, 8), :] * u_ref[x + 1, pl.ds(y - 1, 8), :])
                drive = d_ref[pl.ds((x * EY + 8 * j) * STEPS + step, 8, stride=STEPS), :]
                own = kc_ref[x + 1, pl.ds(y, 8), :] * u - w_ref[x + 1, pl.ds(y, 8), :]
                w_ref[x + 1, pl.ds(y, 8), :] = (own + drive) + ((in_x + in_y) + in_z)

        if step == STEPS - 2:
            prior_copy.start()
    next_copy.start()
    next_copy.wait()
    prior_copy.wait()


def points(place, got):
    tiles = got.shape[0]
    return pl.pallas_call(
        points_kernel,
        out_shape=pltpu.VMEM((ROWS * STEPS, CZ), jnp.float32),
        in_specs=[pl.BlockSpec(memory_space=pltpu.SMEM), vmem_spec()],
        out_specs=vmem_spec(),
        scratch_shapes=[
            pltpu.VMEM((6 * tiles, NPT), jnp.int32),
            pltpu.SMEM((6 * tiles, NPT), jnp.int32),
            pltpu.SMEM((3 * tiles * NPT + 2 * GROUP,), jnp.int32),
            pltpu.SemaphoreType.DMA,
        ],
        cost_estimate=pl.CostEstimate(flops=10**12, transcendentals=0, bytes_accessed=1024 * MIB),
        compiler_params=pltpu.CompilerParams(vmem_limit_bytes=4 * MIB),
    )(place, got.reshape(tiles * PARTS, NPT))


def window(table, drive, fields):
    grid = jax.ShapeDtypeStruct((CX, CY, CZ), jnp.float32)
    buffer = pltpu.VMEM((EX + 2, PY, CZ), jnp.float32)
    return pl.pallas_call(
        window_kernel,
        out_shape=(grid, grid),
        in_specs=[pl.BlockSpec(memory_space=pltpu.SMEM), vmem_spec()] + [any_spec()] * 7,
        out_specs=(any_spec(), any_spec()),
        scratch_shapes=[buffer] * 7 + [
            pltpu.VMEM((CX, CY, CZ), jnp.int32),
            pltpu.SemaphoreType.DMA((3, 5)),
            pltpu.SemaphoreType.DMA((2,)),
        ],
        compiler_params=pltpu.CompilerParams(vmem_limit_bytes=16 * MIB),
    )(table, pltpu.with_memory_space_constraint(drive, pltpu.VMEM), *fields)


def neighbours(low, high, axis):
    count = lax.axis_size(axis)
    up = [(i, i + 1) for i in range(count - 1)]
    down = [(i + 1, i) for i in range(count - 1)]
    return lax.ppermute(high, axis, up), lax.ppermute(low, axis, down)


def shards(field_now, field_before, layer, modulus_table, fk_panel, owner, local_cell):
    sources, tiles = lax.axis_size("along"), lax.axis_size("across")
    local_freqs = fk_panel.shape[1]
    arrays = (field_now, field_before, layer)
    smem = pl.BlockSpec(memory_space=pltpu.SMEM)
    slab = pltpu.VMEM((3 * CX, H, CZ), jnp.float32)
    low, high, dealt = pl.pallas_call(
        prepare_kernel,
        out_shape=(slab, slab, pltpu.VMEM((sources, 2 * local_freqs, NPT), jnp.bfloat16)),
        in_specs=[smem] + [any_spec()] * 3 + [vmem_spec()],
        out_specs=(vmem_spec(),) * 3,
        scratch_shapes=[pltpu.VMEM((2, CX, H, CZ), jnp.int32), pltpu.SemaphoreType.DMA((2, 3))],
        compiler_params=pltpu.CompilerParams(vmem_limit_bytes=58 * MIB),
    )(modulus_table, *arrays, fk_panel.reshape(2, local_freqs, sources * NPT))
    ylo, yhi = neighbours(low, high, "across")
    moved = lax.all_to_all(dealt, "along", 0, 0, tiled=True)
    ylo, yhi, moved = lax.optimization_barrier((ylo, yhi, moved))

    samples = pl.pallas_call(
        transform_kernel,
        out_shape=pltpu.VMEM((2 * STEPS, NPT), jnp.float32),
        in_specs=[vmem_spec()] * 4,
        out_specs=vmem_spec(),
        scratch_shapes=[pltpu.VMEM((2 * local_freqs * sources, NPT), jnp.float32)],
        compiler_params=pltpu.CompilerParams(vmem_limit_bytes=58 * MIB),
    )(moved, jnp.asarray(split_table(sources, local_freqs)), owner.reshape(1, NPT), local_cell)
    left, right = neighbours(samples, samples, "along")
    spread = pl.pallas_call(
        spread_kernel,
        out_shape=pltpu.HBM((tiles, PARTS, NPT), jnp.float32),
        in_specs=[vmem_spec()] * 3,
        out_specs=pl.BlockSpec(memory_space=pltpu.HBM),
        scratch_shapes=[pltpu.VMEM((tiles, PARTS, NPT), jnp.float32), pltpu.SemaphoreType.DMA],
        compiler_params=pltpu.CompilerParams(vmem_limit_bytes=4 * MIB),
    )(samples, left, right)
    got = lax.all_to_all(spread, "across", 0, 0, tiled=True)
    slab = jax.ShapeDtypeStruct((3 * H, EY, CZ), jnp.float32)
    low, high = pl.pallas_call(
        slab_kernel,
        out_shape=(slab, slab),
        in_specs=[smem] + [any_spec()] * 5,
        out_specs=(vmem_spec(),) * 2,
        scratch_shapes=[pltpu.VMEM((2, H, CY, CZ), jnp.int32), pltpu.SemaphoreType.DMA((3, 2, 3))],
        compiler_params=pltpu.CompilerParams(vmem_limit_bytes=58 * MIB),
    )(modulus_table, *arrays, *lax.optimization_barrier((ylo, yhi, samples))[:2])
    xlo, xhi = neighbours(low, high, "along")
    place = lax.axis_index("across").astype(jnp.int32).reshape(1)
    drive = points(place, got)
    return window(modulus_table, drive, (*arrays, ylo, yhi, xlo, xhi))


def solution(mesh):
    placed = (
        P("along", "across", None),
        P("along", "across", None),
        P("along", "across", None),
        P(),
        P(None, "along", "across", None),
        P("across", "along", None),
        P("across", "along"),
    )
    return jax.shard_map(
        shards,
        mesh=mesh,
        in_specs=placed,
        out_specs=(P("along", "across", None), P("along", "across", None)),
        check_vma=False,
    )
```
